128 devices in a mesh: rows: 32 (over x, y, core), cols: 4 (over z).
Axes of the slice: x: 4, y: 4, z: 4, core: 2. Of those that a mesh axis runs over, the one named last changes fastest.
Arguments:
- tiles: bfloat16 [4096, 256, 256], P(('rows', 'cols')), may hold values from -15 to 20
- send_slot: int32 [128, 32], P(('rows', 'cols')), may hold values from 0 to 31, each once within a row
- slot_row: int32 [128, 32], P(('rows', 'cols')), may hold values from 0 to 2, as said below
- slot_fetch: int32 [128, 32], P(('rows', 'cols')), may hold values from 0 to 31
- fetch_list: int32 [128, 32], P(('rows', 'cols')), may hold values from 0 to 1
- basis: bfloat16 [65536, 128], P(('rows', 'cols')), may hold values from -6 to 6
Outputs:
- embedding: bfloat16 [65536, 128], P(('rows', 'cols'))
The draws below stay inside these ranges and needn't reach their ends.
Inputs may be any that keep to these rules, and one draw needn't show every extreme that they name: `slot_row`: value 2 marks an empty slot. Within each block of 8 slots (one source builder) the filled slots come first; some device has all 32 slots filled in every draw.
All inputs are finite; a program needn't handle non-finite values.
Results may differ from the reference program's by a relative error of at most 0.02.
Values may be sent and summed in bfloat16 or wider, within the bound.
A program may use at most 128 MiB of HBM per device.

```python
import jax
import jax.numpy as jnp
from jax import lax

TILE = 256
WIDTH = 128
BR = 2
Q = 8
ITERS = 6
TB = 32
GROUPS = 32
NPTS = 65536
N_COLS = 4
DEVICES = 128


def draw_tiles(key, part):
    shape = (TB * DEVICES, TILE, TILE)
    key_noise = jax.random.fold_in(key, 21)
    noise = jax.random.truncated_normal(key_noise, -6.0, 6.0, shape, jnp.float32)
    values = 0.25 + noise
    return values.astype(jnp.bfloat16)


def draw_slot_row(key, part):
    ncols = TB // Q
    key_count = jax.random.fold_in(key, 11)
    key_full = jax.random.fold_in(key, 12)
    key_row = jax.random.fold_in(key, 13)
    count = jax.random.randint(key_count, (DEVICES, ncols), 1, Q + 1)
    full_dev = jax.random.randint(key_full, (), 0, DEVICES)
    devs = jnp.arange(DEVICES, dtype=jnp.int32)
    count = jnp.where((devs == full_dev)[:, None], Q, count)
    slots = jnp.arange(TB, dtype=jnp.int32)
    filled = slots[None, :] % Q < count[:, slots // Q]
    rows = jax.random.randint(key_row, (DEVICES, TB), 0, BR)
    return jnp.where(filled, rows, BR).astype(jnp.int32)


def set_ends(entries, key, low, top_value):
    longest = entries.shape.index(max(entries.shape))
    spots = []
    for shift in (0, 1):
        where = [jax.random.randint(jax.random.fold_in(key, axis), (), 0, length) for axis, length in enumerate(entries.shape)]
        where[longest] = (where[longest] + shift) % entries.shape[longest]
        spots.append(tuple(where))
    return entries.at[spots[0]].set(low).at[spots[1]].set(top_value)


def level_of(own_key, extent, pieces, smallest, largest):
    def one(dim, shards_of):
        steps = jax.random.uniform(jax.random.fold_in(jax.random.fold_in(own_key, 6), dim), (shards_of,), jnp.float32, smallest / len(pieces), largest / len(pieces))
        return jnp.repeat(jnp.exp(steps), extent[dim] // shards_of).reshape((-1,) + (1,) * (len(extent) - dim - 1))

    factor_of = one(*pieces[0])
    for cut in pieces[1:]:
        factor_of = factor_of * one(*cut)
    return factor_of


def gaussian(stream_key, dims, scale, bound, shards=(), kind=jnp.bfloat16):
    loudness = level_of(stream_key, dims, shards, -0.22, 0.18) if shards else 1.0
    array = jax.random.normal(stream_key, dims, jnp.float32) * scale * loudness
    return jnp.minimum(jnp.maximum(array, -bound), bound).astype(kind)


def setup_inputs(seed: int = 0) -> dict:
    seeds = jax.random.split(jax.random.key(seed), 7)
    return {
        "tiles": draw_tiles(jax.random.fold_in(seeds[6], 71), 0),
        "send_slot": jax.vmap(lambda own: jax.random.permutation(own, TB))(jax.random.split(seeds[1], DEVICES)).reshape((DEVICES, TB)).astype(jnp.int32),
        "slot_row": draw_slot_row(jax.random.fold_in(seeds[6], 71), 0),
        "slot_fetch": set_ends(jax.random.randint(seeds[3], (DEVICES, TB), 0, GROUPS), jax.random.fold_in(seeds[3], 1), 0, GROUPS - 1).astype(jnp.int32),
        "fetch_list": set_ends(jax.random.randint(seeds[4], (DEVICES, GROUPS), 0, BR), jax.random.fold_in(seeds[4], 1), 0, BR - 1).astype(jnp.int32),
        "basis": gaussian(seeds[5], (NPTS, WIDTH), 1.0, 6.0, ((0, 128),)),
    }


def reference(tiles, send_slot, slot_row, slot_fetch, fetch_list, basis):
    devs = slot_row.shape[0]
    slots_all = slot_row.shape[1]
    ncols = N_COLS
    per_src = slots_all // ncols
    npts = basis.shape[0]
    inverse = jnp.argsort(send_slot, axis=1).astype(jnp.int32)
    slots = jnp.arange(slots_all, dtype=jnp.int32)
    owners = jnp.arange(devs, dtype=jnp.int32)
    group = owners // ncols
    column = owners % ncols
    builder = group[:, None] * ncols + slots[None, :] // per_src
    position = column[:, None] * per_src + slots[None, :] % per_src
    source_tile = (builder * slots_all + inverse[builder, position]).astype(jnp.int32)
    wanted = jnp.take_along_axis(fetch_list, slot_fetch, axis=1)
    col_block = ((slot_fetch * ncols + column[:, None]) * BR + wanted).astype(jnp.int32)
    blocks = jnp.arange(BR, dtype=jnp.int32)

    def one_hot(o):
        return (slot_row[o][:, None] == blocks[None, :]).astype(jnp.float32)

    def degree(o):
        weights = tiles[source_tile[o]].astype(jnp.float32)
        row_abs = lax.optimization_barrier(jnp.sum(jnp.abs(weights), axis=2))
        return 1.0 + jnp.dot(one_hot(o).T, row_abs, precision=lax.Precision.HIGHEST)
    deg = lax.map(degree, owners).reshape(npts, 1)
    scale = lax.rsqrt(deg)
    current = basis
    for step in range(ITERS):
        scaled = (scale * current.astype(jnp.float32)).astype(jnp.bfloat16).reshape(devs * BR, TILE, WIDTH)

        def apply(o):
            weights = tiles[source_tile[o]].astype(jnp.float32)
            fetched = scaled[col_block[o]].astype(jnp.float32)
            prod = jnp.einsum('sak,skd->sad', weights, fetched, precision=lax.Precision.HIGHEST)
            return jnp.einsum('sj,sad->jad', one_hot(o), prod, precision=lax.Precision.HIGHEST)
        iterate = lax.map(apply, owners).reshape(npts, WIDTH) * scale
        gram = jnp.dot(iterate.T, iterate, precision=lax.Precision.HIGHEST)
        lower = jnp.linalg.cholesky(gram / npts)
        solved = lax.linalg.triangular_solve(lower, iterate, left_side=False, lower=True, transpose_a=True)
        current = solved.astype(jnp.bfloat16)
    return current
```

```python
import jax
import jax.numpy as jnp
from jax import lax
from jax.experimental import pallas as pl
from jax.experimental.pallas import tpu as pltpu
from jax.sharding import Mesh
from jax.sharding import PartitionSpec as P

TILE = 256
WIDTH = 128
ITERS = 6
NX, NY, NK, NZ = 4, 4, 2, 4
Q = 8
SLOTS = NZ * Q
AXES = ("x", "y", "k", "z")
MESH = pl.DeviceIdType.MESH
HI = lax.Precision.HIGHEST
F32 = jnp.float32
BF16 = jnp.bfloat16


def contract(a, b, da, db, precision=None):
    return lax.dot_general(
        a, b, (((da,), (db,)), ((), ())), precision=precision, preferred_element_type=F32
    )


def kernel(
    meta, tiles, basis, out,
    tin, stg, recv, relay, rsend, rrecv, mrow, scale, gat_even, gat_odd, ybuf, acc,
    gram, zbuf, xbuf, vbuf, gfull, aug, linv,
    in_sem, tile_send, tile_recv, row_send, row_recv,
    ag_send, ag_own, ag_par, ar_send, zsem, xsem, ysem, fsem,
):
    x, y, k, z = (lax.axis_index(a) for a in AXES)
    mod = lax.rem
    xr, xl, xo = mod(x + 1, NX), mod(x + 3, NX), mod(x + 2, NX)
    yr, yl, yo = mod(y + 1, NY), mod(y + 3, NY), mod(y + 2, NY)
    zr, zl, zo = mod(z + 1, NZ), mod(z + 3, NZ), mod(z + 2, NZ)
    kp = 1 - k
    kz_peers = [
        (mod(k + dk, NK), mod(z + dz, NZ))
        for dk in range(NK) for dz in range(NZ) if (dk, dz) != (0, 0)
    ]
    x_peers, y_peers, z_peers = (xr, xl, xo), (yr, yl, yo), (zr, zl, zo)
    me_kz = k * NZ + z

    def remote(src, dst, ssem, rsem, **dev):
        return pltpu.make_async_remote_copy(
            src_ref=src, dst_ref=dst, send_sem=ssem, recv_sem=rsem,
            device_id=dev, device_id_type=MESH,
        )

    load_tiles = pltpu.make_async_copy(tiles, tin, in_sem)
    load_tiles.start()

    barrier = pltpu.get_barrier_semaphore()
    for pk, pz in kz_peers:
        pl.semaphore_signal(barrier, inc=1, device_id={"k": pk, "z": pz}, device_id_type=MESH)
    for px in x_peers:
        pl.semaphore_signal(barrier, inc=1, device_id={"x": px}, device_id_type=MESH)
    for py in y_peers:
        pl.semaphore_signal(barrier, inc=1, device_id={"y": py}, device_id_type=MESH)
    for s in range(SLOTS):
        for j in range(2):
            hit = jnp.where(meta[1, s] == j, 1.0, 0.0).astype(F32)
            mrow[j, s : s + 1, :] = jnp.full((1, WIDTH), hit, F32)
    load_tiles.wait()

    ones = jnp.ones((8, TILE), BF16)

    def stage(d, carry):
        for q in range(Q):
            t = tin[meta[0, d * Q + q]]
            stg[d * Q + q] = t
            rsend[d, q : q + 1, :] = contract(ones, jnp.abs(t), 1, 1)[0:1]
        return carry

    lax.fori_loop(0, NZ, stage, 0)
    pl.semaphore_wait(barrier, len(kz_peers) + len(x_peers) + len(y_peers))

    row_copies = [
        remote(rsend.at[pz], rrecv.at[z], row_send.at[i], row_recv.at[z], z=pz)
        for i, pz in enumerate(z_peers)
    ]
    for c in row_copies:
        c.start()
    half = Q // 2

    def part(start, count):
        return pl.ds(start, count)

    tile_copies = [
        remote(stg.at[part(zo * Q, half)], relay.at[0], tile_send.at[0], tile_recv.at[0], z=zr),
        remote(stg.at[part(zo * Q + half, half)], relay.at[1], tile_send.at[1], tile_recv.at[1], z=zl),
        remote(stg.at[part(zr * Q, Q)], recv.at[part(z * Q, Q)], tile_send.at[2], tile_recv.at[2], z=zr),
        remote(stg.at[part(zl * Q, Q)], recv.at[part(z * Q, Q)], tile_send.at[3], tile_recv.at[3], z=zl),
    ]
    for c in tile_copies:
        c.start()
    for q in range(Q):
        recv[z * Q + q] = stg[z * Q + q]
    rrecv[z] = rsend[z]
    for pz in z_peers:
        pltpu.make_async_copy(rrecv.at[pz], rrecv.at[pz], row_recv.at[pz]).wait()
    for c in row_copies:
        c.wait_send()
    rows = rrecv[...].reshape(SLOTS, TILE)
    for j in range(2):
        scale[j] = lax.rsqrt(1.0 + contract(rows, mrow[j], 0, 0, HI))

    gat = (gat_even, gat_odd)

    def place(flow, core, px, py):
        return ((core * 2 + flow) * NX + px) * NY + py

    def block(par, flow, px, py, piece=None, core=None):
        ref = gat[par].at[place(flow, k if core is None else core, px, py)]
        return ref if piece is None else ref.at[pl.ds(piece * (TILE // 2), TILE // 2)]

    def push(par, flow, px, py, piece=None, **dev):
        ref = block(par, flow, px, py, piece)
        remote(ref, ref, ag_send, ag_own.at[par, flow, px * NY + py], **dev).start()

    def to_partner(par, flow, px, py):
        ref = block(par, flow, px, py)
        remote(ref, ref, ag_send, ag_par.at[par, flow, px * NY + py], k=kp).start()

    def arrived(par, flow, px, py):
        ref = block(par, flow, px, py)
        pltpu.make_async_copy(ref, ref, ag_own.at[par, flow, px * NY + py]).wait()
        to_partner(par, flow, px, py)

    def oriented(flow):
        if flow == 0:
            return (x, xr, xl, xo), (y, yr, yl, yo), "x", "y"
        return (y, yr, yl, yo), (x, xr, xl, xo), "y", "x"

    def at(flow, a, b):
        return (a, b) if flow == 0 else (b, a)

    def gather_own(par):
        for flow in range(2):
            (a, ar, al, ao), (b, br, bl, bo), an, bn = oriented(flow)
            push(par, flow, *at(flow, a, b), **{an: ar})
            push(par, flow, *at(flow, a, b), **{an: al})
        for flow in range(2):
            (a, ar, al, ao), (b, br, bl, bo), an, bn = oriented(flow)
            push(par, flow, *at(flow, a, b), **{bn: br})
            push(par, flow, *at(flow, a, b), **{bn: bl})
        for flow in range(2):
            to_partner(par, flow, x, y)

    def gather_first(par):
        for flow in range(2):
            (a, ar, al, ao), (b, br, bl, bo), an, bn = oriented(flow)
            arrived(par, flow, *at(flow, al, b))
            push(par, flow, *at(flow, al, b), piece=0, **{an: ar})
            push(par, flow, *at(flow, al, b), **{bn: br})
            push(par, flow, *at(flow, al, b), **{bn: bl})
            arrived(par, flow, *at(flow, ar, b))
            push(par, flow, *at(flow, ar, b), piece=1, **{an: al})
            push(par, flow, *at(flow, ar, b), **{bn: br})
            push(par, flow, *at(flow, ar, b), **{bn: bl})

    def across(par, flow, a):
        (_, _, _, _), (b, br, bl, bo), an, bn = oriented(flow)
        arrived(par, flow, *at(flow, a, bl))
        push(par, flow, *at(flow, a, bl), piece=0, **{bn: br})
        arrived(par, flow, *at(flow, a, br))
        push(par, flow, *at(flow, a, br), piece=1, **{bn: bl})

    def gather_second(par):
        for flow in range(2):
            across(par, flow, oriented(flow)[0][0])
        for flow in range(2):
            (a, ar, al, ao), (b, br, bl, bo), an, bn = oriented(flow)
            arrived(par, flow, *at(flow, ao, b))
            push(par, flow, *at(flow, ao, b), **{bn: br})
            push(par, flow, *at(flow, ao, b), **{bn: bl})

    def gather_third(par):
        for flow in range(2):
            (a, ar, al, ao), (b, br, bl, bo), an, bn = oriented(flow)
            across(par, flow, al)
            across(par, flow, ar)
        for flow in range(2):
            (a, ar, al, ao), (b, br, bl, bo), an, bn = oriented(flow)
            arrived(par, flow, *at(flow, a, bo))

    def gather_fourth(par):
        for flow in range(2):
            across(par, flow, oriented(flow)[0][3])

    def gather_end(par):
        for flow in range(2):
            (a, ar, al, ao), (b, br, bl, bo), an, bn = oriented(flow)
            for c in (al, ar, ao):
                arrived(par, flow, *at(flow, c, bo))
        for flow in range(2):
            for px in range(NX):
                for py in range(NY):
                    ref = block(par, flow, px, py, core=kp)
                    pltpu.make_async_copy(ref, ref, ag_par.at[par, flow, px * NY + py]).wait()
        sent = gat[par].at[pl.ds(0, 62)]
        pltpu.make_async_copy(sent, sent, ag_send).wait()

    def set_basis(par, values):
        for j in range(2):
            gat[par][place(j, k, x, y)] = (scale[j] * values[j]).astype(BF16)

    def gram_send(par):
        zbuf[par, me_kz] = gram[me_kz]
        for pk, pz in kz_peers:
            remote(gram.at[pk * NZ + pz], zbuf.at[par, me_kz], ar_send.at[0], zsem.at[par, me_kz], k=pk, z=pz).start()

    def wait_for(ref, sem):
        pltpu.make_async_copy(ref, ref, sem).wait()

    def gram_x(par):
        for pk, pz in kz_peers:
            wait_for(zbuf.at[par, pk * NZ + pz], zsem.at[par, pk * NZ + pz])
        xbuf[par, x] = sum(zbuf[par, i] for i in range(1, NK * NZ)) + zbuf[par, 0]
        for px in x_peers:
            remote(xbuf.at[par, x], xbuf.at[par, x], ar_send.at[1], xsem.at[par, x], x=px).start()

    def gram_y(par):
        for px in x_peers:
            wait_for(xbuf.at[par, px], xsem.at[par, px])
        vbuf[par, y] = (xbuf[par, 0] + xbuf[par, 1]) + (xbuf[par, 2] + xbuf[par, 3])
        for py in y_peers:
            remote(vbuf.at[par, y], vbuf.at[par, y], ar_send.at[2], ysem.at[par, y], y=py).start()

    def gram_all(par):
        for py in y_peers:
            wait_for(vbuf.at[par, py], ysem.at[par, py])
        gfull[par, me_kz] = (vbuf[par, 0] + vbuf[par, 1]) + (vbuf[par, 2] + vbuf[par, 3])
        for pk, pz in kz_peers:
            remote(gfull.at[par, me_kz], gfull.at[par, me_kz], ar_send.at[3], fsem.at[par, me_kz], k=pk, z=pz).start()

    def gram_end(par):
        for pk, pz in kz_peers:
            wait_for(gfull.at[par, pk * NZ + pz], fsem.at[par, pk * NZ + pz])
        wait_for(gram.at[pl.ds(0, 7)], ar_send.at[0])
        wait_for(xbuf.at[par, pl.ds(0, 3)], ar_send.at[1])
        wait_for(vbuf.at[par, pl.ds(0, 3)], ar_send.at[2])
        wait_for(gfull.at[par, pl.ds(0, 7)], ar_send.at[3])

    sub = lax.broadcasted_iota(jnp.int32, (8, 2 * WIDTH), 0)
    npts = NX * NY * NK * NZ * 2 * TILE

    def factor(par):
        aug[:, 0:WIDTH] = gfull[par].reshape(WIDTH, WIDTH) * (1.0 / npts)
        row_id = lax.broadcasted_iota(jnp.int32, (WIDTH, WIDTH), 0)
        col_id = lax.broadcasted_iota(jnp.int32, (WIDTH, WIDTH), 1)
        aug[:, WIDTH:] = jnp.where(row_id == col_id, 1.0, 0.0).astype(F32)
        for p in range(WIDTH // 8):
            rows8 = aug[8 * p : 8 * p + 8, :]
            for j in range(8):
                lane = 8 * p + j
                col = jnp.broadcast_to(rows8[:, lane : lane + 1], (8, 2 * WIDTH))
                pivot = jnp.broadcast_to(col[j : j + 1], (8, 2 * WIDTH))
                row = jnp.broadcast_to(rows8[j : j + 1], (8, 2 * WIDTH))
                inv = lax.rsqrt(pivot)
                row = row * inv
                rows8 = jnp.where(sub > j, rows8 - (col * inv) * row, rows8)
                rows8 = jnp.where(sub == j, row, rows8)
            aug[8 * p : 8 * p + 8, :] = rows8
            if p < WIDTH // 8 - 1:
                update = contract(rows8[:, 0:WIDTH], rows8, 0, 0, HI)
                aug[8 * p + 8 :, :] = aug[8 * p + 8 :, :] - update[8 * p + 8 :, :]
        linv[...] = aug[:, WIDTH:]

    set_basis(0, basis[...].astype(F32).reshape(2, TILE, WIDTH))
    gather_own(0)
    gather_first(0)
    gather_second(0)
    gather_third(0)
    gather_fourth(0)
    for i in range(2):
        wait_for(relay.at[i], tile_recv.at[i])
    passed = [
        remote(relay.at[0], recv.at[part(zl * Q, half)], tile_send.at[4], tile_recv.at[4], z=zr),
        remote(relay.at[1], recv.at[part(zr * Q + half, half)], tile_send.at[5], tile_recv.at[5], z=zl),
    ]
    for c in passed:
        c.start()
    gather_end(0)
    linv[...] = jnp.where(
        lax.broadcasted_iota(jnp.int32, (WIDTH, WIDTH), 0)
        == lax.broadcasted_iota(jnp.int32, (WIDTH, WIDTH), 1), 1.0, 0.0,
    ).astype(F32)
    wait_for(recv.at[part(zl * Q, Q)], tile_recv.at[2])
    wait_for(recv.at[part(zr * Q, Q)], tile_recv.at[3])
    wait_for(recv.at[part(zo * Q, half)], tile_recv.at[4])
    wait_for(recv.at[part(zo * Q + half, half)], tile_recv.at[5])
    for c in tile_copies:
        c.wait_send()
    for c in passed:
        c.wait_send()

    def multiply(par):
        acc[...] = jnp.zeros_like(acc)

        def group(g, carry):
            left, right = [], []
            for q in range(Q):
                s = g * Q + q
                fetch = meta[2, s]
                where = (mod(fetch, 2) * 2 + meta[3, fetch]) * (NX * NY) + fetch // 2
                u = gat[par][where]
                row = meta[1, s]
                zero = jnp.zeros_like(u)
                left.append(recv[s])
                right.append(
                    jnp.concatenate([jnp.where(row == 0, u, zero), jnp.where(row == 1, u, zero)], axis=1)
                )
            acc[...] += jnp.dot(
                jnp.concatenate(left, axis=1), jnp.concatenate(right, axis=0),
                preferred_element_type=F32,
            )
            return carry

        lax.fori_loop(0, NZ, group, 0)

    def iteration(now, more):
        later = 1 - now
        multiply(now)
        for j in range(2):
            ybuf[j] = contract(scale[j] * acc[:, j * WIDTH : (j + 1) * WIDTH], linv[...], 1, 1, HI)
        local = contract(ybuf[0], ybuf[0], 0, 0, HI) + contract(ybuf[1], ybuf[1], 0, 0, HI)
        gram[...] = local.reshape(NK * NZ, WIDTH // (NK * NZ), WIDTH)

        def when_more(body):
            if more is True:
                body()
            else:
                pl.when(more)(body)

        when_more(lambda: set_basis(later, ybuf))
        gram_send(later)

        def first():
            gather_own(later)
            gather_first(later)

        when_more(first)
        gram_x(later)
        when_more(lambda: gather_second(later))
        gram_y(later)
        gram_all(later)

        def last():
            gather_third(later)
            gather_fourth(later)

        when_more(last)
        gram_end(later)
        factor(later)
        when_more(lambda: gather_end(later))

    def pair(i, carry):
        iteration(0, True)
        iteration(1, i < ITERS // 2 - 1)
        return carry

    lax.fori_loop(0, ITERS // 2, pair, 0)
    for j in range(2):
        out[j * TILE : (j + 1) * TILE, :] = contract(ybuf[j], linv[...], 1, 1, HI).astype(BF16)


def on_device(tiles, send_slot, slot_row, slot_fetch, fetch_list, basis):
    slots = jnp.arange(SLOTS, dtype=jnp.int32)
    hit = send_slot[0][None, :] == slots[:, None]
    inverse = jnp.sum(jnp.where(hit, slots[None, :], 0), axis=1, dtype=jnp.int32)
    meta = jnp.concatenate([inverse[None], slot_row, slot_fetch, fetch_list], axis=0)
    dma = pltpu.SemaphoreType.DMA
    vmem = pltpu.VMEM
    chunk = WIDTH // (NK * NZ)
    return pl.pallas_call(
        kernel,
        out_shape=jax.ShapeDtypeStruct(basis.shape, BF16),
        in_specs=[
            pl.BlockSpec(memory_space=pltpu.SMEM),
            pl.BlockSpec(memory_space=pl.ANY),
            pl.BlockSpec(memory_space=pltpu.VMEM),
        ],
        out_specs=pl.BlockSpec(memory_space=pltpu.VMEM),
        scratch_shapes=[
            vmem((SLOTS, TILE, TILE), BF16),
            vmem((SLOTS, TILE, TILE), BF16),
            vmem((SLOTS, TILE, TILE), BF16),
            vmem((2, Q // 2, TILE, TILE), BF16),
            vmem((NZ, Q, TILE), F32),
            vmem((NZ, Q, TILE), F32),
            vmem((2, SLOTS, WIDTH), F32),
            vmem((2, TILE, WIDTH), F32),
            vmem((2 * NX * NY * NK, TILE, WIDTH), BF16),
            vmem((2 * NX * NY * NK, TILE, WIDTH), BF16),
            vmem((2, TILE, WIDTH), F32),
            vmem((TILE, 2 * WIDTH), F32),
            vmem((NK * NZ, chunk, WIDTH), F32),
            vmem((2, NK * NZ, chunk, WIDTH), F32),
            vmem((2, NX, chunk, WIDTH), F32),
            vmem((2, NY, chunk, WIDTH), F32),
            vmem((2, NK * NZ, chunk, WIDTH), F32),
            vmem((WIDTH, 2 * WIDTH), F32),
            vmem((WIDTH, WIDTH), F32),
            dma, dma((6,)), dma((6,)), dma((NZ - 1,)), dma((NZ,)),
            dma, dma((2, 2, NX * NY)), dma((2, 2, NX * NY)),
            dma((4,)), dma((2, NK * NZ)), dma((2, NX)), dma((2, NY)), dma((2, NK * NZ)),
        ],
        compiler_params=pltpu.CompilerParams(collective_id=0, has_side_effects=True),
    )(meta, tiles, basis)


def solution(mesh):
    split = Mesh(mesh.devices.reshape(NX, NY, NK, NZ), AXES)
    return jax.shard_map(
        on_device,
        mesh=split,
        in_specs=(P(AXES, None, None),) + (P(AXES, None),) * 5,
        out_specs=P(AXES, None),
        check_vma=False,
    )
```

```python
import jax
import jax.numpy as jnp
from jax import lax
from jax.experimental import pallas as pl
from jax.experimental.pallas import tpu as pltpu
from jax.sharding import Mesh
from jax.sharding import PartitionSpec as P

TILE = 256
WIDTH = 128
ITERS = 6
NX, NY, NK, NZ = 4, 4, 2, 4
Q = 8
SLOTS = NZ * Q
AXES = ("x", "y", "k", "z")
MESH = pl.DeviceIdType.MESH
HI = lax.Precision.HIGHEST
F32 = jnp.float32
BF16 = jnp.bfloat16


def contract(a, b, da, db, precision=None):
    return lax.dot_general(
        a, b, (((da,), (db,)), ((), ())), precision=precision, preferred_element_type=F32
    )


def kernel(
    meta, tiles, basis, out,
    tin, stg, recv, relay, rsend, rrecv, mrow, scale, gat_even, gat_odd, ybuf, acc,
    gram, zbuf, xbuf, vbuf, gfull, aug, linv,
    in_sem, tile_send, tile_recv, row_send, row_recv,
    ag_send, ag_own, ag_par, ar_send, zsem, xsem, ysem, fsem,
):
    x, y, k, z = (lax.axis_index(a) for a in AXES)
    mod = lax.rem
    xr, xl, xo = mod(x + 1, NX), mod(x + 3, NX), mod(x + 2, NX)
    yr, yl, yo = mod(y + 1, NY), mod(y + 3, NY), mod(y + 2, NY)
    zr, zl, zo = mod(z + 1, NZ), mod(z + 3, NZ), mod(z + 2, NZ)
    kp = 1 - k
    kz_peers = [
        (mod(k + dk, NK), mod(z + dz, NZ))
        for dk in range(NK) for dz in range(NZ) if (dk, dz) != (0, 0)
    ]
    x_peers, y_peers, z_peers = (xr, xl, xo), (yr, yl, yo), (zr, zl, zo)
    me_kz = k * NZ + z

    def remote(src, dst, ssem, rsem, **dev):
        return pltpu.make_async_remote_copy(
            src_ref=src, dst_ref=dst, send_sem=ssem, recv_sem=rsem,
            device_id=dev, device_id_type=MESH,
        )

    load_tiles = pltpu.make_async_copy(tiles, tin, in_sem)
    load_tiles.start()

    barrier = pltpu.get_barrier_semaphore()
    for pk, pz in kz_peers:
        pl.semaphore_signal(barrier, inc=1, device_id={"k": pk, "z": pz}, device_id_type=MESH)
    for px in x_peers:
        pl.semaphore_signal(barrier, inc=1, device_id={"x": px}, device_id_type=MESH)
    for py in y_peers:
        pl.semaphore_signal(barrier, inc=1, device_id={"y": py}, device_id_type=MESH)
    for s in range(SLOTS):
        for j in range(2):
            hit = jnp.where(meta[1, s] == j, 1.0, 0.0).astype(F32)
            mrow[j, s : s + 1, :] = jnp.full((1, WIDTH), hit, F32)
    load_tiles.wait()

    ones = jnp.ones((8, TILE), BF16)

    def stage(d, carry):
        for q in range(Q):
            t = tin[meta[0, d * Q + q]]
            stg[d * Q + q] = t
            rsend[d, q : q + 1, :] = contract(ones, jnp.abs(t), 1, 1)[0:1]
        return carry

    lax.fori_loop(0, NZ, stage, 0)
    pl.semaphore_wait(barrier, len(kz_peers) + len(x_peers) + len(y_peers))

    row_copies = [
        remote(rsend.at[pz], rrecv.at[z], row_send.at[i], row_recv.at[z], z=pz)
        for i, pz in enumerate(z_peers)
    ]
    for c in row_copies:
        c.start()
    half = Q // 2

    def part(start, count):
        return pl.ds(start, count)

    tile_copies = [
        remote(stg.at[part(zo * Q, half)], relay.at[0], tile_send.at[0], tile_recv.at[0], z=zr),
        remote(stg.at[part(zo * Q + half, half)], relay.at[1], tile_send.at[1], tile_recv.at[1], z=zl),
        remote(stg.at[part(zr * Q, Q)], recv.at[part(z * Q, Q)], tile_send.at[2], tile_recv.at[2], z=zr),
        remote(stg.at[part(zl * Q, Q)], recv.at[part(z * Q, Q)], tile_send.at[3], tile_recv.at[3], z=zl),
    ]
    for c in tile_copies:
        c.start()
    for q in range(Q):
        recv[z * Q + q] = stg[z * Q + q]
    rrecv[z] = rsend[z]
    for pz in z_peers:
        pltpu.make_async_copy(rrecv.at[pz], rrecv.at[pz], row_recv.at[pz]).wait()
    for c in row_copies:
        c.wait_send()
    rows = rrecv[...].reshape(SLOTS, TILE)
    for j in range(2):
        scale[j] = lax.rsqrt(1.0 + contract(rows, mrow[j], 0, 0, HI))

    gat = (gat_even, gat_odd)

    def place(flow, core, px, py):
        return ((core * 2 + flow) * NX + px) * NY + py

    def block(par, flow, px, py, piece=None, core=None):
        ref = gat[par].at[place(flow, k if core is None else core, px, py)]
        return ref if piece is None else ref.at[pl.ds(piece * (TILE // 2), TILE // 2)]

    def push(par, flow, px, py, piece=None, **dev):
        ref = block(par, flow, px, py, piece)
        remote(ref, ref, ag_send, ag_own.at[par, flow, px * NY + py], **dev).start()

    def to_partner(par, flow, px, py):
        ref = block(par, flow, px, py)
        remote(ref, ref, ag_send, ag_par.at[par, flow, px * NY + py], k=kp).start()

    def arrived(par, flow, px, py):
        ref = block(par, flow, px, py)
        pltpu.make_async_copy(ref, ref, ag_own.at[par, flow, px * NY + py]).wait()
        to_partner(par, flow, px, py)

    def oriented(flow):
        if flow == 0:
            return (x, xr, xl, xo), (y, yr, yl, yo), "x", "y"
        return (y, yr, yl, yo), (x, xr, xl, xo), "y", "x"

    def at(flow, a, b):
        return (a, b) if flow == 0 else (b, a)

    def gather_own(par):
        for flow in range(2):
            (a, ar, al, ao), (b, br, bl, bo), an, bn = oriented(flow)
            push(par, flow, *at(flow, a, b), **{an: ar})
            push(par, flow, *at(flow, a, b), **{an: al})
        for flow in range(2):
            (a, ar, al, ao), (b, br, bl, bo), an, bn = oriented(flow)
            push(par, flow, *at(flow, a, b), **{bn: br})
            push(par, flow, *at(flow, a, b), **{bn: bl})
        for flow in range(2):
            to_partner(par, flow, x, y)

    def gather_first(par):
        for flow in range(2):
            (a, ar, al, ao), (b, br, bl, bo), an, bn = oriented(flow)
            arrived(par, flow, *at(flow, al, b))
            push(par, flow, *at(flow, al, b), piece=0, **{an: ar})
            push(par, flow, *at(flow, al, b), **{bn: br})
            push(par, flow, *at(flow, al, b), **{bn: bl})
            arrived(par, flow, *at(flow, ar, b))
            push(par, flow, *at(flow, ar, b), piece=1, **{an: al})
            push(par, flow, *at(flow, ar, b), **{bn: br})
            push(par, flow, *at(flow, ar, b), **{bn: bl})

    def across(par, flow, a):
        (_, _, _, _), (b, br, bl, bo), an, bn = oriented(flow)
        arrived(par, flow, *at(flow, a, bl))
        push(par, flow, *at(flow, a, bl), piece=0, **{bn: br})
        arrived(par, flow, *at(flow, a, br))
        push(par, flow, *at(flow, a, br), piece=1, **{bn: bl})

    def gather_second(par):
        for flow in range(2):
            across(par, flow, oriented(flow)[0][0])
        for flow in range(2):
            (a, ar, al, ao), (b, br, bl, bo), an, bn = oriented(flow)
            arrived(par, flow, *at(flow, ao, b))
            push(par, flow, *at(flow, ao, b), **{bn: br})
            push(par, flow, *at(flow, ao, b), **{bn: bl})

    def gather_third(par):
        for flow in range(2):
            (a, ar, al, ao), (b, br, bl, bo), an, bn = oriented(flow)
            across(par, flow, al)
            across(par, flow, ar)
        for flow in range(2):
            (a, ar, al, ao), (b, br, bl, bo), an, bn = oriented(flow)
            arrived(par, flow, *at(flow, a, bo))

    def gather_fourth(par):
        for flow in range(2):
            across(par, flow, oriented(flow)[0][3])

    def gather_end(par):
        for flow in range(2):
            (a, ar, al, ao), (b, br, bl, bo), an, bn = oriented(flow)
            for c in (al, ar, ao):
                arrived(par, flow, *at(flow, c, bo))
        for flow in range(2):
            for px in range(NX):
                for py in range(NY):
                    ref = block(par, flow, px, py, core=kp)
                    pltpu.make_async_copy(ref, ref, ag_par.at[par, flow, px * NY + py]).wait()
        sent = gat[par].at[pl.ds(0, 62)]
        pltpu.make_async_copy(sent, sent, ag_send).wait()

    def set_basis(par, values):
        for j in range(2):
            gat[par][place(j, k, x, y)] = (scale[j] * values[j]).astype(BF16)

    def gram_send(par):
        zbuf[par, me_kz] = gram[me_kz]
        for pk, pz in kz_peers:
            remote(gram.at[pk * NZ + pz], zbuf.at[par, me_kz], ar_send.at[0], zsem.at[par, me_kz], k=pk, z=pz).start()

    def wait_for(ref, sem):
        pltpu.make_async_copy(ref, ref, sem).wait()

    def gram_x(par):
        for pk, pz in kz_peers:
            wait_for(zbuf.at[par, pk * NZ + pz], zsem.at[par, pk * NZ + pz])
        xbuf[par, x] = sum(zbuf[par, i] for i in range(1, NK * NZ)) + zbuf[par, 0]
        for px in x_peers:
            remote(xbuf.at[par, x], xbuf.at[par, x], ar_send.at[1], xsem.at[par, x], x=px).start()

    def gram_y(par):
        for px in x_peers:
            wait_for(xbuf.at[par, px], xsem.at[par, px])
        vbuf[par, y] = (xbuf[par, 0] + xbuf[par, 1]) + (xbuf[par, 2] + xbuf[par, 3])
        for py in y_peers:
            remote(vbuf.at[par, y], vbuf.at[par, y], ar_send.at[2], ysem.at[par, y], y=py).start()

    def gram_all(par):
        for py in y_peers:
            wait_for(vbuf.at[par, py], ysem.at[par, py])
        gfull[par, me_kz] = (vbuf[par, 0] + vbuf[par, 1]) + (vbuf[par, 2] + vbuf[par, 3])
        for pk, pz in kz_peers:
            remote(gfull.at[par, me_kz], gfull.at[par, me_kz], ar_send.at[3], fsem.at[par, me_kz], k=pk, z=pz).start()

    def gram_end(par):
        for pk, pz in kz_peers:
            wait_for(gfull.at[par, pk * NZ + pz], fsem.at[par, pk * NZ + pz])
        wait_for(gram.at[pl.ds(0, 7)], ar_send.at[0])
        wait_for(xbuf.at[par, pl.ds(0, 3)], ar_send.at[1])
        wait_for(vbuf.at[par, pl.ds(0, 3)], ar_send.at[2])
        wait_for(gfull.at[par, pl.ds(0, 7)], ar_send.at[3])

    npts = NX * NY * NK * NZ * 2 * TILE
    panel = 16
    lane_id = lax.broadcasted_iota(jnp.int32, (WIDTH, WIDTH), 1)
    row_id = lax.broadcasted_iota(jnp.int32, (WIDTH, WIDTH), 0)
    sub_id = lax.broadcasted_iota(jnp.int32, (8, WIDTH), 0)

    def outer(rows):
        high = rows.astype(BF16)
        rest = rows - high.astype(F32)
        mid = rest.astype(BF16)
        low = (rest - mid.astype(F32)).astype(BF16)
        a = jnp.concatenate([high, high, mid, mid, high, low], axis=0)
        b = jnp.concatenate([high, mid, high, mid, low, high], axis=0)
        return contract(a[:, 0:WIDTH], b, 0, 0)

    def eliminate(base):
        rows = [aug[pl.ds(base + r, 8, stride=0), :] for r in range(panel)]
        d = {
            (r, c): jnp.broadcast_to(rows[r][:, base + c : base + c + 1], (8, WIDTH))
            for r in range(panel) for c in range(r, panel)
        }
        inv, low = [], {}
        for j in range(panel):
            inv.append(lax.rsqrt(d[j, j]))
            for c in range(j + 1, panel):
                low[c, j] = d[j, c] * inv[j]
            for r in range(j + 1, panel):
                for c in range(r, panel):
                    d[r, c] = d[r, c] - low[r, j] * low[c, j]
        done = []
        for j in range(panel):
            left, right = rows[j][:, 0:WIDTH], rows[j][:, WIDTH:]
            for i in range(j):
                left = left - low[j, i] * done[i][0]
                right = right - low[j, i] * done[i][1]
            done.append((left * inv[j], right * inv[j]))
        groups = []
        for o in range(0, panel, 8):
            sides = []
            for side in range(2):
                v = done[o][side]
                for j in range(1, 8):
                    v = jnp.where(sub_id == j, done[o + j][side], v)
                sides.append(v)
            groups.append(jnp.concatenate(sides, axis=1))
        return jnp.concatenate(groups, axis=0)

    def factor(par):
        aug[:, 0:WIDTH] = gfull[par].reshape(WIDTH, WIDTH) * (1.0 / npts)
        aug[:, WIDTH:] = jnp.where(row_id == lane_id, 1.0, 0.0).astype(F32)
        for base in range(0, WIDTH, panel):
            rows = eliminate(base)
            aug[base : base + panel, :] = rows
            after = base + panel
            if after < WIDTH:
                aug[after:, :] = aug[after:, :] - outer(rows)[after:, :]
        linv[...] = aug[:, WIDTH:]

    set_basis(0, basis[...].astype(F32).reshape(2, TILE, WIDTH))
    gather_own(0)
    gather_first(0)
    gather_second(0)
    gather_third(0)
    gather_fourth(0)
    for i in range(2):
        wait_for(relay.at[i], tile_recv.at[i])
    passed = [
        remote(relay.at[0], recv.at[part(zl * Q, half)], tile_send.at[4], tile_recv.at[4], z=zr),
        remote(relay.at[1], recv.at[part(zr * Q + half, half)], tile_send.at[5], tile_recv.at[5], z=zl),
    ]
    for c in passed:
        c.start()
    gather_end(0)
    linv[...] = jnp.where(
        lax.broadcasted_iota(jnp.int32, (WIDTH, WIDTH), 0)
        == lax.broadcasted_iota(jnp.int32, (WIDTH, WIDTH), 1), 1.0, 0.0,
    ).astype(F32)
    wait_for(recv.at[part(zl * Q, Q)], tile_recv.at[2])
    wait_for(recv.at[part(zr * Q, Q)], tile_recv.at[3])
    wait_for(recv.at[part(zo * Q, half)], tile_recv.at[4])
    wait_for(recv.at[part(zo * Q + half, half)], tile_recv.at[5])
    for c in tile_copies:
        c.wait_send()
    for c in passed:
        c.wait_send()

    def multiply(par):
        acc[...] = jnp.zeros_like(acc)

        def group(g, carry):
            left, right = [], []
            for q in range(Q):
                s = g * Q + q
                fetch = meta[2, s]
                where = (mod(fetch, 2) * 2 + meta[3, fetch]) * (NX * NY) + fetch // 2
                u = gat[par][where]
                row = meta[1, s]
                zero = jnp.zeros_like(u)
                left.append(recv[s])
                right.append(
                    jnp.concatenate([jnp.where(row == 0, u, zero), jnp.where(row == 1, u, zero)], axis=1)
                )
            acc[...] += jnp.dot(
                jnp.concatenate(left, axis=1), jnp.concatenate(right, axis=0),
                preferred_element_type=F32,
            )
            return carry

        lax.fori_loop(0, NZ, group, 0)

    def iteration(now, more):
        later = 1 - now
        multiply(now)
        for j in range(2):
            ybuf[j] = contract(scale[j] * acc[:, j * WIDTH : (j + 1) * WIDTH], linv[...], 1, 1, HI)
        local = contract(ybuf[0], ybuf[0], 0, 0, HI) + contract(ybuf[1], ybuf[1], 0, 0, HI)
        gram[...] = local.reshape(NK * NZ, WIDTH // (NK * NZ), WIDTH)

        def when_more(body):
            if more is True:
                body()
            else:
                pl.when(more)(body)

        when_more(lambda: set_basis(later, ybuf))
        gram_send(later)

        def first():
            gather_own(later)
            gather_first(later)

        when_more(first)
        gram_x(later)
        when_more(lambda: gather_second(later))
        gram_y(later)
        gram_all(later)

        def last():
            gather_third(later)
            gather_fourth(later)

        when_more(last)
        gram_end(later)
        factor(later)
        when_more(lambda: gather_end(later))

    def pair(i, carry):
        iteration(0, True)
        iteration(1, i < ITERS // 2 - 1)
        return carry

    lax.fori_loop(0, ITERS // 2, pair, 0)
    for j in range(2):
        out[j * TILE : (j + 1) * TILE, :] = contract(ybuf[j], linv[...], 1, 1, HI).astype(BF16)


def on_device(tiles, send_slot, slot_row, slot_fetch, fetch_list, basis):
    slots = jnp.arange(SLOTS, dtype=jnp.int32)
    hit = send_slot[0][None, :] == slots[:, None]
    inverse = jnp.sum(jnp.where(hit, slots[None, :], 0), axis=1, dtype=jnp.int32)
    meta = jnp.concatenate([inverse[None], slot_row, slot_fetch, fetch_list], axis=0)
    dma = pltpu.SemaphoreType.DMA
    vmem = pltpu.VMEM
    chunk = WIDTH // (NK * NZ)
    return pl.pallas_call(
        kernel,
        out_shape=jax.ShapeDtypeStruct(basis.shape, BF16),
        in_specs=[
            pl.BlockSpec(memory_space=pltpu.SMEM),
            pl.BlockSpec(memory_space=pl.ANY),
            pl.BlockSpec(memory_space=pltpu.VMEM),
        ],
        out_specs=pl.BlockSpec(memory_space=pltpu.VMEM),
        scratch_shapes=[
            vmem((SLOTS, TILE, TILE), BF16),
            vmem((SLOTS, TILE, TILE), BF16),
            vmem((SLOTS, TILE, TILE), BF16),
            vmem((2, Q // 2, TILE, TILE), BF16),
            vmem((NZ, Q, TILE), F32),
            vmem((NZ, Q, TILE), F32),
            vmem((2, SLOTS, WIDTH), F32),
            vmem((2, TILE, WIDTH), F32),
            vmem((2 * NX * NY * NK, TILE, WIDTH), BF16),
            vmem((2 * NX * NY * NK, TILE, WIDTH), BF16),
            vmem((2, TILE, WIDTH), F32),
            vmem((TILE, 2 * WIDTH), F32),
            vmem((NK * NZ, chunk, WIDTH), F32),
            vmem((2, NK * NZ, chunk, WIDTH), F32),
            vmem((2, NX, chunk, WIDTH), F32),
            vmem((2, NY, chunk, WIDTH), F32),
            vmem((2, NK * NZ, chunk, WIDTH), F32),
            vmem((WIDTH, 2 * WIDTH), F32),
            vmem((WIDTH, WIDTH), F32),
            dma, dma((6,)), dma((6,)), dma((NZ - 1,)), dma((NZ,)),
            dma, dma((2, 2, NX * NY)), dma((2, 2, NX * NY)),
            dma((4,)), dma((2, NK * NZ)), dma((2, NX)), dma((2, NY)), dma((2, NK * NZ)),
        ],
        compiler_params=pltpu.CompilerParams(collective_id=0, has_side_effects=True),
    )(meta, tiles, basis)


def solution(mesh):
    split = Mesh(mesh.devices.reshape(NX, NY, NK, NZ), AXES)
    return jax.shard_map(
        on_device,
        mesh=split,
        in_specs=(P(AXES, None, None),) + (P(AXES, None),) * 5,
        out_specs=P(AXES, None),
        check_vma=False,
    )
```

```python
import functools

import jax
import jax.numpy as jnp
from jax import lax
from jax.experimental import pallas as pl
from jax.experimental.pallas import tpu as pltpu
from jax.sharding import Mesh
from jax.sharding import PartitionSpec as P

TILE = 256
WIDTH = 128
ITERS = 6
NX, NY, NK, NZ = 4, 4, 2, 4
Q = 8
SLOTS = NZ * Q
AXES = ("x", "y", "k", "z")
MESH = pl.DeviceIdType.MESH
HI = lax.Precision.HIGHEST
F32 = jnp.float32
BF16 = jnp.bfloat16
ORDER = (
    "basis", "send", "own", "plane", "on1", "on2", "on3", "x0", "all",
    "x1", "x2", "x3", "sum", "factor", "last", "end",
)


def contract(a, b, da, db, precision=None):
    return lax.dot_general(
        a, b, (((da,), (db,)), ((), ())), precision=precision, preferred_element_type=F32
    )


def kernel(
    meta, tiles, basis, out,
    tin, stg, recv, relay, rsend, rrecv, mrow, scale, gat_even, gat_odd, ybuf, acc,
    gram, zbuf, xybuf, gfull, aug, linv,
    in_sem, tile_send, tile_recv, row_send, row_recv,
    ag_send, ag_own, ag_par, ar_send, zsem, xysem, fsem,
):
    x, y, k, z = (lax.axis_index(a) for a in AXES)
    mod = lax.rem
    xr, xl, xo = mod(x + 1, NX), mod(x + 3, NX), mod(x + 2, NX)
    yr, yl, yo = mod(y + 1, NY), mod(y + 3, NY), mod(y + 2, NY)
    zr, zl, zo = mod(z + 1, NZ), mod(z + 3, NZ), mod(z + 2, NZ)
    kp = 1 - k
    kz_peers = [
        (mod(k + dk, NK), mod(z + dz, NZ))
        for dz in (2, 1, 3, 0) for dk in (1, 0) if (dk, dz) != (0, 0)
    ]
    xy_peers = [
        (mod(x + dx, NX), mod(y + dy, NY))
        for dx in (2, 1, 3, 0) for dy in (2, 1, 3, 0) if (dx, dy) != (0, 0)
    ]
    z_peers = (zo, zr, zl)
    me_xy = x * NY + y
    me_kz = k * NZ + z

    def remote(src, dst, ssem, rsem, **dev):
        return pltpu.make_async_remote_copy(
            src_ref=src, dst_ref=dst, send_sem=ssem, recv_sem=rsem,
            device_id=dev, device_id_type=MESH,
        )

    load_tiles = pltpu.make_async_copy(tiles, tin, in_sem)
    load_tiles.start()

    barrier = pltpu.get_barrier_semaphore()
    for pk, pz in kz_peers:
        pl.semaphore_signal(barrier, inc=1, device_id={"k": pk, "z": pz}, device_id_type=MESH)
    for px, py in xy_peers:
        pl.semaphore_signal(barrier, inc=1, device_id={"x": px, "y": py}, device_id_type=MESH)
    for s in range(SLOTS):
        for j in range(2):
            hit = jnp.where(meta[1, s] == j, 1.0, 0.0).astype(F32)
            mrow[j, s : s + 1, :] = jnp.full((1, WIDTH), hit, F32)
    load_tiles.wait()

    ones = jnp.ones((8, TILE), BF16)

    def stage(d, carry):
        for q in range(Q):
            t = tin[meta[0, d * Q + q]]
            stg[d * Q + q] = t
            rsend[d, q : q + 1, :] = contract(ones, jnp.abs(t), 1, 1)[0:1]
        return carry

    lax.fori_loop(0, NZ, stage, 0)
    pl.semaphore_wait(barrier, len(kz_peers) + len(xy_peers))

    row_copies = [
        remote(rsend.at[pz], rrecv.at[z], row_send.at[i], row_recv.at[z], z=pz)
        for i, pz in enumerate(z_peers)
    ]
    for c in row_copies:
        c.start()
    half = Q // 2

    def part(start, count):
        return pl.ds(start, count)

    tile_copies = [
        remote(stg.at[part(zo * Q, half)], relay.at[0], tile_send.at[0], tile_recv.at[0], z=zr),
        remote(stg.at[part(zo * Q + half, half)], relay.at[1], tile_send.at[1], tile_recv.at[1], z=zl),
        remote(stg.at[part(zr * Q, Q)], recv.at[part(z * Q, Q)], tile_send.at[2], tile_recv.at[2], z=zr),
        remote(stg.at[part(zl * Q, Q)], recv.at[part(z * Q, Q)], tile_send.at[3], tile_recv.at[3], z=zl),
    ]
    for c in tile_copies:
        c.start()
    for q in range(Q):
        recv[z * Q + q] = stg[z * Q + q]
    rrecv[z] = rsend[z]
    for pz in z_peers:
        pltpu.make_async_copy(rrecv.at[pz], rrecv.at[pz], row_recv.at[pz]).wait()
    for c in row_copies:
        c.wait_send()
    rows = rrecv[...].reshape(SLOTS, TILE)
    for j in range(2):
        scale[j] = lax.rsqrt(1.0 + contract(rows, mrow[j], 0, 0, HI))

    gat = (gat_even, gat_odd)

    def place(flow, core, px, py):
        return ((core * 2 + flow) * NX + px) * NY + py

    def block(par, flow, px, py, piece=None, core=None):
        ref = gat[par].at[place(flow, k if core is None else core, px, py)]
        return ref if piece is None else ref.at[pl.ds(piece * (TILE // 2), TILE // 2)]

    def push(par, flow, px, py, piece=None, **dev):
        ref = block(par, flow, px, py, piece)
        remote(ref, ref, ag_send, ag_own.at[par, flow, px * NY + py], **dev).start()

    def to_partner(par, flow, px, py):
        ref = block(par, flow, px, py)
        remote(ref, ref, ag_send, ag_par.at[par, flow, px * NY + py], k=kp).start()

    def arrived(par, flow, px, py):
        ref = block(par, flow, px, py)
        pltpu.make_async_copy(ref, ref, ag_own.at[par, flow, px * NY + py]).wait()
        to_partner(par, flow, px, py)

    def oriented(flow):
        if flow == 0:
            return (x, xr, xl, xo), (y, yr, yl, yo), "x", "y"
        return (y, yr, yl, yo), (x, xr, xl, xo), "y", "x"

    def at(flow, a, b):
        return (a, b) if flow == 0 else (b, a)

    def gather_own(par):
        for flow in range(2):
            (a, ar, al, ao), (b, br, bl, bo), an, bn = oriented(flow)
            for c in (ao, ar, al):
                push(par, flow, *at(flow, a, b), **{an: c})
        for flow in range(2):
            (a, ar, al, ao), (b, br, bl, bo), an, bn = oriented(flow)
            for c in (br, bl):
                push(par, flow, *at(flow, a, b), **{bn: c})
        for flow in range(2):
            to_partner(par, flow, x, y)

    def onward(par, hop):
        for flow in range(2):
            firsts, (b, br, bl, bo), an, bn = oriented(flow)
            arrived(par, flow, *at(flow, firsts[hop], b))
            for c in (br, bl):
                push(par, flow, *at(flow, firsts[hop], b), **{bn: c})

    def across(par, hop):
        for flow in range(2):
            firsts, (b, br, bl, bo), an, bn = oriented(flow)
            a = firsts[hop]
            arrived(par, flow, *at(flow, a, bl))
            push(par, flow, *at(flow, a, bl), piece=0, **{bn: br})
            arrived(par, flow, *at(flow, a, br))
            push(par, flow, *at(flow, a, br), piece=1, **{bn: bl})

    def gather_last(par):
        for hop in range(4):
            for flow in range(2):
                firsts, (b, br, bl, bo), an, bn = oriented(flow)
                arrived(par, flow, *at(flow, firsts[hop], bo))

    def gather_end(par):
        for flow in range(2):
            for px in range(NX):
                for py in range(NY):
                    ref = block(par, flow, px, py, core=kp)
                    pltpu.make_async_copy(ref, ref, ag_par.at[par, flow, px * NY + py]).wait()
        sent = gat[par].at[pl.ds(0, 62)]
        pltpu.make_async_copy(sent, sent, ag_send).wait()

    def set_basis(par, values):
        for j in range(2):
            gat[par][place(j, k, x, y)] = (scale[j] * values[j]).astype(BF16)

    def total(buf, par, count):
        terms = [buf[par, i] for i in range(count)]
        while len(terms) > 1:
            terms = [terms[i] + terms[i + 1] for i in range(0, len(terms), 2)]
        return terms[0]

    def gram_send(par):
        zbuf[par, me_kz] = gram[me_kz]
        for pk, pz in kz_peers:
            remote(gram.at[pk * NZ + pz], zbuf.at[par, me_kz], ar_send.at[0], zsem.at[par, me_kz], k=pk, z=pz).start()

    def wait_for(ref, sem):
        pltpu.make_async_copy(ref, ref, sem).wait()

    def gram_plane(par):
        for pk, pz in kz_peers:
            wait_for(zbuf.at[par, pk * NZ + pz], zsem.at[par, pk * NZ + pz])
        xybuf[par, me_xy] = total(zbuf, par, NK * NZ)
        for px, py in xy_peers:
            mine = xybuf.at[par, me_xy]
            remote(mine, mine, ar_send.at[1], xysem.at[par, me_xy], x=px, y=py).start()

    def gram_all(par):
        for px, py in xy_peers:
            wait_for(xybuf.at[par, px * NY + py], xysem.at[par, px * NY + py])
        gfull[par, me_kz] = total(xybuf, par, NX * NY)
        for pk, pz in kz_peers:
            mine = gfull.at[par, me_kz]
            remote(mine, mine, ar_send.at[2], fsem.at[par, me_kz], k=pk, z=pz).start()

    def gram_end(par):
        for pk, pz in kz_peers:
            wait_for(gfull.at[par, pk * NZ + pz], fsem.at[par, pk * NZ + pz])
        wait_for(gram.at[pl.ds(0, 7)], ar_send.at[0])
        wait_for(xybuf.at[par, pl.ds(0, 15)], ar_send.at[1])
        wait_for(gfull.at[par, pl.ds(0, 7)], ar_send.at[2])

    npts = NX * NY * NK * NZ * 2 * TILE
    panel = 16
    lane_id = lax.broadcasted_iota(jnp.int32, (WIDTH, WIDTH), 1)
    row_id = lax.broadcasted_iota(jnp.int32, (WIDTH, WIDTH), 0)
    sub_id = lax.broadcasted_iota(jnp.int32, (8, WIDTH), 0)

    def outer(rows):
        high = rows.astype(BF16)
        rest = rows - high.astype(F32)
        mid = rest.astype(BF16)
        low = (rest - mid.astype(F32)).astype(BF16)
        a = jnp.concatenate([high, high, mid, mid, high, low], axis=0)
        b = jnp.concatenate([high, mid, high, mid, low, high], axis=0)
        return contract(a[:, 0:WIDTH], b, 0, 0)

    def eliminate(base):
        rows = [aug[pl.ds(base + r, 8, stride=0), :] for r in range(panel)]
        d = {
            (r, c): jnp.broadcast_to(rows[r][:, base + c : base + c + 1], (8, WIDTH))
            for r in range(panel) for c in range(r, panel)
        }
        inv, low = [], {}
        for j in range(panel):
            inv.append(lax.rsqrt(d[j, j]))
            for c in range(j + 1, panel):
                low[c, j] = d[j, c] * inv[j]
            for r in range(j + 1, panel):
                for c in range(r, panel):
                    d[r, c] = d[r, c] - low[r, j] * low[c, j]
        done = []
        for j in range(panel):
            left, right = rows[j][:, 0:WIDTH], rows[j][:, WIDTH:]
            for i in range(j):
                left = left - low[j, i] * done[i][0]
                right = right - low[j, i] * done[i][1]
            done.append((left * inv[j], right * inv[j]))
        groups = []
        for o in range(0, panel, 8):
            sides = []
            for side in range(2):
                v = done[o][side]
                for j in range(1, 8):
                    v = jnp.where(sub_id == j, done[o + j][side], v)
                sides.append(v)
            groups.append(jnp.concatenate(sides, axis=1))
        return jnp.concatenate(groups, axis=0)

    def factor(par):
        aug[:, 0:WIDTH] = gfull[par].reshape(WIDTH, WIDTH) * (1.0 / npts)
        aug[:, WIDTH:] = jnp.where(row_id == lane_id, 1.0, 0.0).astype(F32)
        for base in range(0, WIDTH, panel):
            rows = eliminate(base)
            aug[base : base + panel, :] = rows
            after = base + panel
            if after < WIDTH:
                aug[after:, :] = aug[after:, :] - outer(rows)[after:, :]
        linv[...] = aug[:, WIDTH:]

    set_basis(0, basis[...].astype(F32).reshape(2, TILE, WIDTH))
    gather_own(0)
    for hop in (1, 2, 3):
        onward(0, hop)
    for hop in range(4):
        across(0, hop)
    gather_last(0)
    for i in range(2):
        wait_for(relay.at[i], tile_recv.at[i])
    passed = [
        remote(relay.at[0], recv.at[part(zl * Q, half)], tile_send.at[4], tile_recv.at[4], z=zr),
        remote(relay.at[1], recv.at[part(zr * Q + half, half)], tile_send.at[5], tile_recv.at[5], z=zl),
    ]
    for c in passed:
        c.start()
    gather_end(0)
    linv[...] = jnp.where(
        lax.broadcasted_iota(jnp.int32, (WIDTH, WIDTH), 0)
        == lax.broadcasted_iota(jnp.int32, (WIDTH, WIDTH), 1), 1.0, 0.0,
    ).astype(F32)
    wait_for(recv.at[part(zl * Q, Q)], tile_recv.at[2])
    wait_for(recv.at[part(zr * Q, Q)], tile_recv.at[3])
    wait_for(recv.at[part(zo * Q, half)], tile_recv.at[4])
    wait_for(recv.at[part(zo * Q + half, half)], tile_recv.at[5])
    for c in tile_copies:
        c.wait_send()
    for c in passed:
        c.wait_send()

    def multiply(par):
        acc[...] = jnp.zeros_like(acc)

        def group(g, carry):
            left, right = [], []
            for q in range(Q):
                s = g * Q + q
                fetch = meta[2, s]
                where = (mod(fetch, 2) * 2 + meta[3, fetch]) * (NX * NY) + fetch // 2
                u = gat[par][where]
                row = meta[1, s]
                zero = jnp.zeros_like(u)
                left.append(recv[s])
                right.append(
                    jnp.concatenate([jnp.where(row == 0, u, zero), jnp.where(row == 1, u, zero)], axis=1)
                )
            acc[...] += jnp.dot(
                jnp.concatenate(left, axis=1), jnp.concatenate(right, axis=0),
                preferred_element_type=F32,
            )
            return carry

        lax.fori_loop(0, NZ, group, 0)

    def iteration(now, more):
        later = 1 - now
        multiply(now)
        for j in range(2):
            ybuf[j] = contract(scale[j] * acc[:, j * WIDTH : (j + 1) * WIDTH], linv[...], 1, 1, HI)
        local = contract(ybuf[0], ybuf[0], 0, 0, HI) + contract(ybuf[1], ybuf[1], 0, 0, HI)
        gram[...] = local.reshape(NK * NZ, WIDTH // (NK * NZ), WIDTH)

        def when_more(body):
            if more is True:
                body()
            else:
                pl.when(more)(body)

        steps = {
            "basis": lambda: set_basis(later, ybuf),
            "own": lambda: gather_own(later),
            "last": lambda: gather_last(later),
            "end": lambda: gather_end(later),
        }
        for hop in range(4):
            steps[f"on{hop}"] = functools.partial(onward, later, hop)
            steps[f"x{hop}"] = functools.partial(across, later, hop)
        sums = {
            "send": gram_send, "plane": gram_plane, "all": gram_all, "sum": gram_end, "factor": factor,
        }
        waiting = []

        def flush():
            todo = list(waiting)
            waiting.clear()

            def body():
                for name in todo:
                    steps[name]()

            if todo:
                when_more(body)

        for name in ORDER:
            if name in sums:
                flush()
                sums[name](later)
            else:
                waiting.append(name)
        flush()

    def pair(i, carry):
        iteration(0, True)
        iteration(1, i < ITERS // 2 - 1)
        return carry

    lax.fori_loop(0, ITERS // 2, pair, 0)
    for j in range(2):
        out[j * TILE : (j + 1) * TILE, :] = contract(ybuf[j], linv[...], 1, 1, HI).astype(BF16)


def on_device(tiles, send_slot, slot_row, slot_fetch, fetch_list, basis):
    slots = jnp.arange(SLOTS, dtype=jnp.int32)
    hit = send_slot[0][None, :] == slots[:, None]
    inverse = jnp.sum(jnp.where(hit, slots[None, :], 0), axis=1, dtype=jnp.int32)
    meta = jnp.concatenate([inverse[None], slot_row, slot_fetch, fetch_list], axis=0)
    dma = pltpu.SemaphoreType.DMA
    vmem = pltpu.VMEM
    chunk = WIDTH // (NK * NZ)
    return pl.pallas_call(
        kernel,
        out_shape=jax.ShapeDtypeStruct(basis.shape, BF16),
        in_specs=[
            pl.BlockSpec(memory_space=pltpu.SMEM),
            pl.BlockSpec(memory_space=pl.ANY),
            pl.BlockSpec(memory_space=pltpu.VMEM),
        ],
        out_specs=pl.BlockSpec(memory_space=pltpu.VMEM),
        scratch_shapes=[
            vmem((SLOTS, TILE, TILE), BF16),
            vmem((SLOTS, TILE, TILE), BF16),
            vmem((SLOTS, TILE, TILE), BF16),
            vmem((2, Q // 2, TILE, TILE), BF16),
            vmem((NZ, Q, TILE), F32),
            vmem((NZ, Q, TILE), F32),
            vmem((2, SLOTS, WIDTH), F32),
            vmem((2, TILE, WIDTH), F32),
            vmem((2 * NX * NY * NK, TILE, WIDTH), BF16),
            vmem((2 * NX * NY * NK, TILE, WIDTH), BF16),
            vmem((2, TILE, WIDTH), F32),
            vmem((TILE, 2 * WIDTH), F32),
            vmem((NK * NZ, chunk, WIDTH), F32),
            vmem((2, NK * NZ, chunk, WIDTH), F32),
            vmem((2, NX * NY, chunk, WIDTH), F32),
            vmem((2, NK * NZ, chunk, WIDTH), F32),
            vmem((WIDTH, 2 * WIDTH), F32),
            vmem((WIDTH, WIDTH), F32),
            dma, dma((6,)), dma((6,)), dma((NZ - 1,)), dma((NZ,)),
            dma, dma((2, 2, NX * NY)), dma((2, 2, NX * NY)),
            dma((3,)), dma((2, NK * NZ)), dma((2, NX * NY)), dma((2, NK * NZ)),
        ],
        compiler_params=pltpu.CompilerParams(collective_id=0, has_side_effects=True),
    )(meta, tiles, basis)


def solution(mesh):
    split = Mesh(mesh.devices.reshape(NX, NY, NK, NZ), AXES)
    return jax.shard_map(
        on_device,
        mesh=split,
        in_specs=(P(AXES, None, None),) + (P(AXES, None),) * 5,
        out_specs=P(AXES, None),
        check_vma=False,
    )
```

```python
import functools

import jax
import jax.numpy as jnp
from jax import lax
from jax.experimental import pallas as pl
from jax.experimental.pallas import tpu as pltpu
from jax.sharding import Mesh
from jax.sharding import PartitionSpec as P

TILE = 256
WIDTH = 128
ITERS = 6
NX, NY, NK, NZ = 4, 4, 2, 4
Q = 8
SLOTS = NZ * Q
AXES = ("x", "y", "k", "z")
MESH = pl.DeviceIdType.MESH
HI = lax.Precision.HIGHEST
F32 = jnp.float32
BF16 = jnp.bfloat16
ORDER = (
    "basis", "send", "own", "plane", "on1", "on2", "on3", "x0", "all",
    "x1", "x2", "x3", "sum", "top", "last", "rest", "end",
)
SPLIT = 80


def contract(a, b, da, db, precision=None):
    return lax.dot_general(
        a, b, (((da,), (db,)), ((), ())), precision=precision, preferred_element_type=F32
    )


def kernel(
    send_slot, slot_row, slot_fetch, fetch_list, tiles, basis, out,
    source, tin, stg, recv, rsend, rrecv, mrow, scale, gat_even, gat_odd, ybuf, acc,
    gram, zbuf, xybuf, gfull, aug, linv,
    in_sem, tile_send, tile_recv, row_send, row_recv,
    ag_send, ag_own, ag_par, ar_send, zsem, xysem, fsem,
):
    x, y, k, z = (lax.axis_index(a) for a in AXES)
    mod = lax.rem
    xr, xl, xo = mod(x + 1, NX), mod(x + 3, NX), mod(x + 2, NX)
    yr, yl, yo = mod(y + 1, NY), mod(y + 3, NY), mod(y + 2, NY)
    zr, zl, zo = mod(z + 1, NZ), mod(z + 3, NZ), mod(z + 2, NZ)
    kp = 1 - k
    kz_peers = [
        (mod(k + dk, NK), mod(z + dz, NZ))
        for dz in (2, 1, 3, 0) for dk in (1, 0) if (dk, dz) != (0, 0)
    ]
    xy_peers = [
        (mod(x + dx, NX), mod(y + dy, NY))
        for dx in (2, 1, 3, 0) for dy in (2, 1, 3, 0) if (dx, dy) != (0, 0)
    ]
    z_peers = (zo, zr, zl)
    me_xy = x * NY + y
    me_kz = k * NZ + z

    def remote(src, dst, ssem, rsem, **dev):
        return pltpu.make_async_remote_copy(
            src_ref=src, dst_ref=dst, send_sem=ssem, recv_sem=rsem,
            device_id=dev, device_id_type=MESH,
        )

    load_tiles = pltpu.make_async_copy(tiles, tin, in_sem)
    load_tiles.start()

    barrier = pltpu.get_barrier_semaphore()
    for pk, pz in kz_peers:
        pl.semaphore_signal(barrier, inc=1, device_id={"k": pk, "z": pz}, device_id_type=MESH)
    for px, py in xy_peers:
        pl.semaphore_signal(barrier, inc=1, device_id={"x": px, "y": py}, device_id_type=MESH)

    def find_tile(slot, carry):
        tile = jnp.int32(0)
        for t in range(SLOTS):
            tile = jnp.where(send_slot[0, t] == slot, t, tile)
        source[slot] = tile
        return carry

    lax.fori_loop(0, SLOTS, find_tile, 0)
    for s in range(SLOTS):
        for j in range(2):
            hit = jnp.where(slot_row[0, s] == j, 1.0, 0.0).astype(F32)
            mrow[j, s : s + 1, :] = jnp.full((1, WIDTH), hit, F32)
    load_tiles.wait()

    ones = jnp.ones((8, TILE), BF16)

    def part(start, count):
        return pl.ds(start, count)

    def put_in_order(d):
        for q in range(Q):
            stg[d * Q + q] = tin[source[d * Q + q]]

    def send_tiles(i, pz, first, count):
        c = remote(
            stg.at[part(pz * Q + first, count)], recv.at[part(z * Q + first, count)],
            tile_send.at[i], tile_recv.at[z], z=pz,
        )
        c.start()
        return c

    few = 2
    put_in_order(zr)
    put_in_order(zl)
    pl.semaphore_wait(barrier, len(kz_peers) + len(xy_peers))
    tile_copies = [send_tiles(0, zr, 0, few), send_tiles(1, zl, 0, few)]
    put_in_order(zo)
    put_in_order(z)

    def sum_rows(d, carry):
        for q in range(Q):
            t = jnp.abs(stg[d * Q + q])
            rsend[d, q : q + 1, :] = contract(ones, t, 1, 1)[0:1]
        return carry

    lax.fori_loop(0, NZ, sum_rows, 0)
    row_copies = [
        remote(rsend.at[pz], rrecv.at[z], row_send.at[i], row_recv.at[z], z=pz)
        for i, pz in enumerate(z_peers)
    ]
    for c in row_copies:
        c.start()
    tile_copies += [
        send_tiles(2, zo, 0, Q), send_tiles(3, zr, few, Q - few), send_tiles(4, zl, few, Q - few)
    ]
    for q in range(Q):
        recv[z * Q + q] = stg[z * Q + q]
    rrecv[z] = rsend[z]
    for pz in z_peers:
        pltpu.make_async_copy(rrecv.at[pz], rrecv.at[pz], row_recv.at[pz]).wait()
    for c in row_copies:
        c.wait_send()
    rows = rrecv[...].reshape(SLOTS, TILE)
    for j in range(2):
        scale[j] = lax.rsqrt(1.0 + contract(rows, mrow[j], 0, 0, HI))

    gat = (gat_even, gat_odd)

    def place(flow, core, px, py):
        return ((core * 2 + flow) * NX + px) * NY + py

    def block(par, flow, px, py, piece=None, core=None):
        ref = gat[par].at[place(flow, k if core is None else core, px, py)]
        return ref if piece is None else ref.at[pl.ds(piece * (TILE // 2), TILE // 2)]

    def push(par, flow, px, py, piece=None, **dev):
        ref = block(par, flow, px, py, piece)
        remote(ref, ref, ag_send, ag_own.at[par, flow, px * NY + py], **dev).start()

    def to_partner(par, flow, px, py):
        ref = block(par, flow, px, py)
        remote(ref, ref, ag_send, ag_par.at[par, flow, px * NY + py], k=kp).start()

    def arrived(par, flow, px, py):
        ref = block(par, flow, px, py)
        pltpu.make_async_copy(ref, ref, ag_own.at[par, flow, px * NY + py]).wait()
        to_partner(par, flow, px, py)

    def oriented(flow):
        if flow == 0:
            return (x, xr, xl, xo), (y, yr, yl, yo), "x", "y"
        return (y, yr, yl, yo), (x, xr, xl, xo), "y", "x"

    def at(flow, a, b):
        return (a, b) if flow == 0 else (b, a)

    def gather_own(par):
        for flow in range(2):
            (a, ar, al, ao), (b, br, bl, bo), an, bn = oriented(flow)
            for c in (ao, ar, al):
                push(par, flow, *at(flow, a, b), **{an: c})
        for flow in range(2):
            (a, ar, al, ao), (b, br, bl, bo), an, bn = oriented(flow)
            for c in (br, bl):
                push(par, flow, *at(flow, a, b), **{bn: c})
        for flow in range(2):
            to_partner(par, flow, x, y)

    def onward(par, hop):
        for flow in range(2):
            firsts, (b, br, bl, bo), an, bn = oriented(flow)
            arrived(par, flow, *at(flow, firsts[hop], b))
            for c in (br, bl):
                push(par, flow, *at(flow, firsts[hop], b), **{bn: c})

    def across(par, hop):
        for flow in range(2):
            firsts, (b, br, bl, bo), an, bn = oriented(flow)
            a = firsts[hop]
            arrived(par, flow, *at(flow, a, bl))
            push(par, flow, *at(flow, a, bl), piece=0, **{bn: br})
            arrived(par, flow, *at(flow, a, br))
            push(par, flow, *at(flow, a, br), piece=1, **{bn: bl})

    def gather_last(par):
        for hop in range(4):
            for flow in range(2):
                firsts, (b, br, bl, bo), an, bn = oriented(flow)
                arrived(par, flow, *at(flow, firsts[hop], bo))

    def gather_end(par):
        for flow in range(2):
            for px in range(NX):
                for py in range(NY):
                    ref = block(par, flow, px, py, core=kp)
                    pltpu.make_async_copy(ref, ref, ag_par.at[par, flow, px * NY + py]).wait()
        sent = gat[par].at[pl.ds(0, 62)]
        pltpu.make_async_copy(sent, sent, ag_send).wait()

    def set_basis(par, values):
        for j in range(2):
            gat[par][place(j, k, x, y)] = (scale[j] * values[j]).astype(BF16)

    def total(buf, par, count):
        terms = [buf[par, i] for i in range(count)]
        while len(terms) > 1:
            terms = [terms[i] + terms[i + 1] for i in range(0, len(terms), 2)]
        return terms[0]

    def gram_send(par):
        zbuf[par, me_kz] = gram[me_kz]
        for pk, pz in kz_peers:
            remote(gram.at[pk * NZ + pz], zbuf.at[par, me_kz], ar_send.at[0], zsem.at[par, me_kz], k=pk, z=pz).start()

    def wait_for(ref, sem):
        pltpu.make_async_copy(ref, ref, sem).wait()

    def gram_plane(par):
        for pk, pz in kz_peers:
            wait_for(zbuf.at[par, pk * NZ + pz], zsem.at[par, pk * NZ + pz])
        xybuf[par, me_xy] = total(zbuf, par, NK * NZ)
        for px, py in xy_peers:
            mine = xybuf.at[par, me_xy]
            remote(mine, mine, ar_send.at[1], xysem.at[par, me_xy], x=px, y=py).start()

    def gram_all(par):
        for px, py in xy_peers:
            wait_for(xybuf.at[par, px * NY + py], xysem.at[par, px * NY + py])
        gfull[par, me_kz] = total(xybuf, par, NX * NY)
        for pk, pz in kz_peers:
            mine = gfull.at[par, me_kz]
            remote(mine, mine, ar_send.at[2], fsem.at[par, me_kz], k=pk, z=pz).start()

    def gram_end(par):
        for pk, pz in kz_peers:
            wait_for(gfull.at[par, pk * NZ + pz], fsem.at[par, pk * NZ + pz])
        wait_for(gram.at[pl.ds(0, 7)], ar_send.at[0])
        wait_for(xybuf.at[par, pl.ds(0, 15)], ar_send.at[1])
        wait_for(gfull.at[par, pl.ds(0, 7)], ar_send.at[2])

    npts = NX * NY * NK * NZ * 2 * TILE
    panel = 16
    lane_id = lax.broadcasted_iota(jnp.int32, (WIDTH, WIDTH), 1)
    row_id = lax.broadcasted_iota(jnp.int32, (WIDTH, WIDTH), 0)
    sub_id = lax.broadcasted_iota(jnp.int32, (8, WIDTH), 0)

    def outer(rows):
        high = rows.astype(BF16)
        rest = rows - high.astype(F32)
        mid = rest.astype(BF16)
        low = (rest - mid.astype(F32)).astype(BF16)
        a = jnp.concatenate([high, high, mid, mid, high, low], axis=0)
        b = jnp.concatenate([high, mid, high, mid, low, high], axis=0)
        return contract(a[:, 0:WIDTH], b, 0, 0)

    def eliminate(base):
        rows = [aug[pl.ds(base + r, 8, stride=0), :] for r in range(panel)]
        d = {
            (r, c): jnp.broadcast_to(rows[r][:, base + c : base + c + 1], (8, WIDTH))
            for r in range(panel) for c in range(r, panel)
        }
        inv, low = [], {}
        for j in range(panel):
            inv.append(lax.rsqrt(d[j, j]))
            for c in range(j + 1, panel):
                low[c, j] = d[j, c] * inv[j]
            for r in range(j + 1, panel):
                for c in range(r, panel):
                    d[r, c] = d[r, c] - low[r, j] * low[c, j]
        done = []
        for j in range(panel):
            left, right = rows[j][:, 0:WIDTH], rows[j][:, WIDTH:]
            for i in range(j):
                left = left - low[j, i] * done[i][0]
                right = right - low[j, i] * done[i][1]
            done.append((left * inv[j], right * inv[j]))
        groups = []
        for o in range(0, panel, 8):
            sides = []
            for side in range(2):
                v = done[o][side]
                for j in range(1, 8):
                    v = jnp.where(sub_id == j, done[o + j][side], v)
                sides.append(v)
            groups.append(jnp.concatenate(sides, axis=1))
        return jnp.concatenate(groups, axis=0)

    def eliminate_rows(first, last):
        for base in range(first, last, panel):
            rows = eliminate(base)
            aug[base : base + panel, :] = rows
            after = base + panel
            if after < WIDTH:
                aug[after:, :] = aug[after:, :] - outer(rows)[after:, :]

    def factor_top(par):
        aug[:, 0:WIDTH] = gfull[par].reshape(WIDTH, WIDTH) * (1.0 / npts)
        aug[:, WIDTH:] = jnp.where(row_id == lane_id, 1.0, 0.0).astype(F32)
        eliminate_rows(0, SPLIT)

    def factor_rest(par):
        eliminate_rows(SPLIT, WIDTH)
        linv[...] = aug[:, WIDTH:]

    set_basis(0, basis[...].astype(F32).reshape(2, TILE, WIDTH))
    gather_own(0)
    for hop in (1, 2, 3):
        onward(0, hop)
    for hop in range(4):
        across(0, hop)
    gather_last(0)
    gather_end(0)
    linv[...] = jnp.where(
        lax.broadcasted_iota(jnp.int32, (WIDTH, WIDTH), 0)
        == lax.broadcasted_iota(jnp.int32, (WIDTH, WIDTH), 1), 1.0, 0.0,
    ).astype(F32)
    for pz in z_peers:
        wait_for(recv.at[part(pz * Q, Q)], tile_recv.at[pz])
    for c in tile_copies:
        c.wait_send()

    def multiply(par):
        acc[...] = jnp.zeros_like(acc)

        def group(g, carry):
            left, right = [], []
            for q in range(Q):
                s = g * Q + q
                fetch = slot_fetch[0, s]
                where = (mod(fetch, 2) * 2 + fetch_list[0, fetch]) * (NX * NY) + fetch // 2
                u = gat[par][where]
                row = slot_row[0, s]
                zero = jnp.zeros_like(u)
                left.append(recv[s])
                right.append(
                    jnp.concatenate([jnp.where(row == 0, u, zero), jnp.where(row == 1, u, zero)], axis=1)
                )
            acc[...] += jnp.dot(
                jnp.concatenate(left, axis=1), jnp.concatenate(right, axis=0),
                preferred_element_type=F32,
            )
            return carry

        lax.fori_loop(0, NZ, group, 0)

    def iteration(now, more):
        later = 1 - now
        multiply(now)
        for j in range(2):
            ybuf[j] = contract(scale[j] * acc[:, j * WIDTH : (j + 1) * WIDTH], linv[...], 1, 1, HI)
        local = contract(ybuf[0], ybuf[0], 0, 0, HI) + contract(ybuf[1], ybuf[1], 0, 0, HI)
        gram[...] = local.reshape(NK * NZ, WIDTH // (NK * NZ), WIDTH)

        def when_more(body):
            if more is True:
                body()
            else:
                pl.when(more)(body)

        steps = {
            "basis": lambda: set_basis(later, ybuf),
            "own": lambda: gather_own(later),
            "last": lambda: gather_last(later),
            "end": lambda: gather_end(later),
        }
        for hop in range(4):
            steps[f"on{hop}"] = functools.partial(onward, later, hop)
            steps[f"x{hop}"] = functools.partial(across, later, hop)
        sums = {
            "send": gram_send, "plane": gram_plane, "all": gram_all, "sum": gram_end,
            "top": factor_top, "rest": factor_rest,
        }
        waiting = []

        def flush():
            todo = list(waiting)
            waiting.clear()

            def body():
                for name in todo:
                    steps[name]()

            if todo:
                when_more(body)

        for name in ORDER:
            if name in sums:
                flush()
                sums[name](later)
            else:
                waiting.append(name)
        flush()

    def pair(i, carry):
        iteration(0, True)
        iteration(1, i < ITERS // 2 - 1)
        return carry

    lax.fori_loop(0, ITERS // 2, pair, 0)
    for j in range(2):
        out[j * TILE : (j + 1) * TILE, :] = contract(ybuf[j], linv[...], 1, 1, HI).astype(BF16)


def on_device(tiles, send_slot, slot_row, slot_fetch, fetch_list, basis):
    dma = pltpu.SemaphoreType.DMA
    vmem = pltpu.VMEM
    chunk = WIDTH // (NK * NZ)
    return pl.pallas_call(
        kernel,
        out_shape=jax.ShapeDtypeStruct(basis.shape, BF16),
        in_specs=[
            pl.BlockSpec(memory_space=pltpu.SMEM),
            pl.BlockSpec(memory_space=pltpu.SMEM),
            pl.BlockSpec(memory_space=pltpu.SMEM),
            pl.BlockSpec(memory_space=pltpu.SMEM),
            pl.BlockSpec(memory_space=pl.ANY),
            pl.BlockSpec(memory_space=pltpu.VMEM),
        ],
        out_specs=pl.BlockSpec(memory_space=pltpu.VMEM),
        scratch_shapes=[
            pltpu.SMEM((SLOTS,), jnp.int32),
            vmem((SLOTS, TILE, TILE), BF16),
            vmem((SLOTS, TILE, TILE), BF16),
            vmem((SLOTS, TILE, TILE), BF16),
            vmem((NZ, Q, TILE), F32),
            vmem((NZ, Q, TILE), F32),
            vmem((2, SLOTS, WIDTH), F32),
            vmem((2, TILE, WIDTH), F32),
            vmem((2 * NX * NY * NK, TILE, WIDTH), BF16),
            vmem((2 * NX * NY * NK, TILE, WIDTH), BF16),
            vmem((2, TILE, WIDTH), F32),
            vmem((TILE, 2 * WIDTH), F32),
            vmem((NK * NZ, chunk, WIDTH), F32),
            vmem((2, NK * NZ, chunk, WIDTH), F32),
            vmem((2, NX * NY, chunk, WIDTH), F32),
            vmem((2, NK * NZ, chunk, WIDTH), F32),
            vmem((WIDTH, 2 * WIDTH), F32),
            vmem((WIDTH, WIDTH), F32),
            dma, dma((5,)), dma((NZ,)), dma((NZ - 1,)), dma((NZ,)),
            dma, dma((2, 2, NX * NY)), dma((2, 2, NX * NY)),
            dma((3,)), dma((2, NK * NZ)), dma((2, NX * NY)), dma((2, NK * NZ)),
        ],
        compiler_params=pltpu.CompilerParams(collective_id=0, has_side_effects=True),
    )(send_slot, slot_row, slot_fetch, fetch_list, tiles, basis)


def solution(mesh):
    split = Mesh(mesh.devices.reshape(NX, NY, NK, NZ), AXES)
    return jax.shard_map(
        on_device,
        mesh=split,
        in_specs=(P(AXES, None, None),) + (P(AXES, None),) * 5,
        out_specs=P(AXES, None),
        check_vma=False,
    )
```

```python
import functools

import jax
import jax.numpy as jnp
from jax import lax
from jax.experimental import pallas as pl
from jax.experimental.pallas import tpu as pltpu
from jax.sharding import Mesh
from jax.sharding import PartitionSpec as P

TILE = 256
WIDTH = 128
ITERS = 6
NX, NY, NK, NZ = 4, 4, 2, 4
Q = 8
SLOTS = NZ * Q
AXES = ("x", "y", "k", "z")
MESH = pl.DeviceIdType.MESH
HI = lax.Precision.HIGHEST
F32 = jnp.float32
BF16 = jnp.bfloat16
ORDER = (
    "basis", "send", "own", "plane", "on1", "on2", "on3", "x0", "all",
    "x1", "x2", "x3", "sum", "top", "last", "middle",
)
SPLITS = (80, 112)


def contract(a, b, da, db, precision=None):
    return lax.dot_general(
        a, b, (((da,), (db,)), ((), ())), precision=precision, preferred_element_type=F32
    )


def kernel(
    send_slot, slot_row, slot_fetch, fetch_list, tiles, basis, out,
    source, tin, stg, recv, rsend, rrecv, mrow, scale, gat_even, gat_odd, ybuf, acc,
    gram, zbuf, xybuf, gfull, aug, linv,
    in_sem, tile_send, tile_recv, row_send, row_recv,
    ag_send, ag_own, ag_par, ar_send, zsem, xysem, fsem,
):
    x, y, k, z = (lax.axis_index(a) for a in AXES)
    mod = lax.rem
    xr, xl, xo = mod(x + 1, NX), mod(x + 3, NX), mod(x + 2, NX)
    yr, yl, yo = mod(y + 1, NY), mod(y + 3, NY), mod(y + 2, NY)
    zr, zl, zo = mod(z + 1, NZ), mod(z + 3, NZ), mod(z + 2, NZ)
    kp = 1 - k
    kz_peers = [
        (mod(k + dk, NK), mod(z + dz, NZ))
        for dz in (2, 1, 3, 0) for dk in (1, 0) if (dk, dz) != (0, 0)
    ]
    xy_peers = [
        (mod(x + dx, NX), mod(y + dy, NY))
        for dx in (2, 1, 3, 0) for dy in (2, 1, 3, 0) if (dx, dy) != (0, 0)
    ]
    z_peers = (zo, zr, zl)
    me_xy = x * NY + y
    me_kz = k * NZ + z

    def remote(src, dst, ssem, rsem, **dev):
        return pltpu.make_async_remote_copy(
            src_ref=src, dst_ref=dst, send_sem=ssem, recv_sem=rsem,
            device_id=dev, device_id_type=MESH,
        )

    load_tiles = pltpu.make_async_copy(tiles, tin, in_sem)
    load_tiles.start()

    barrier = pltpu.get_barrier_semaphore()
    for pk, pz in kz_peers:
        pl.semaphore_signal(barrier, inc=1, device_id={"k": pk, "z": pz}, device_id_type=MESH)
    for px, py in xy_peers:
        pl.semaphore_signal(barrier, inc=1, device_id={"x": px, "y": py}, device_id_type=MESH)

    def find_tile(slot, carry):
        tile = jnp.int32(0)
        for t in range(SLOTS):
            tile = jnp.where(send_slot[0, t] == slot, t, tile)
        source[slot] = tile
        return carry

    lax.fori_loop(0, SLOTS, find_tile, 0)
    for s in range(SLOTS):
        for j in range(2):
            hit = jnp.where(slot_row[0, s] == j, 1.0, 0.0).astype(F32)
            mrow[j, s : s + 1, :] = jnp.full((1, WIDTH), hit, F32)
    load_tiles.wait()

    ones = jnp.ones((8, TILE), BF16)

    def part(start, count):
        return pl.ds(start, count)

    def put_in_order(d):
        for q in range(Q):
            stg[d * Q + q] = tin[source[d * Q + q]]

    def send_tiles(i, pz, first, count):
        c = remote(
            stg.at[part(pz * Q + first, count)], recv.at[part(z * Q + first, count)],
            tile_send.at[i], tile_recv.at[z], z=pz,
        )
        c.start()
        return c

    few = 2
    put_in_order(zr)
    put_in_order(zl)
    pl.semaphore_wait(barrier, len(kz_peers) + len(xy_peers))
    tile_copies = [send_tiles(0, zr, 0, few), send_tiles(1, zl, 0, few)]
    put_in_order(zo)
    put_in_order(z)

    def sum_rows(d, carry):
        for q in range(Q):
            t = jnp.abs(stg[d * Q + q])
            rsend[d, q : q + 1, :] = contract(ones, t, 1, 1)[0:1]
        return carry

    lax.fori_loop(0, NZ, sum_rows, 0)
    row_copies = [
        remote(rsend.at[pz], rrecv.at[z], row_send.at[i], row_recv.at[z], z=pz)
        for i, pz in enumerate(z_peers)
    ]
    for c in row_copies:
        c.start()
    tile_copies += [
        send_tiles(2, zo, 0, Q), send_tiles(3, zr, few, Q - few), send_tiles(4, zl, few, Q - few)
    ]
    for q in range(Q):
        recv[z * Q + q] = stg[z * Q + q]
    rrecv[z] = rsend[z]
    for pz in z_peers:
        pltpu.make_async_copy(rrecv.at[pz], rrecv.at[pz], row_recv.at[pz]).wait()
    for c in row_copies:
        c.wait_send()
    rows = rrecv[...].reshape(SLOTS, TILE)
    for j in range(2):
        scale[j] = lax.rsqrt(1.0 + contract(rows, mrow[j], 0, 0, HI))

    gat = (gat_even, gat_odd)

    def place(flow, core, px, py):
        return ((core * 2 + flow) * NX + px) * NY + py

    def block(par, flow, px, py, piece=None, core=None):
        ref = gat[par].at[place(flow, k if core is None else core, px, py)]
        return ref if piece is None else ref.at[pl.ds(piece * (TILE // 2), TILE // 2)]

    def push(par, flow, px, py, piece=None, **dev):
        ref = block(par, flow, px, py, piece)
        remote(ref, ref, ag_send, ag_own.at[par, flow, px * NY + py], **dev).start()

    def to_partner(par, flow, px, py):
        ref = block(par, flow, px, py)
        remote(ref, ref, ag_send, ag_par.at[par, flow, px * NY + py], k=kp).start()

    def arrived(par, flow, px, py):
        ref = block(par, flow, px, py)
        pltpu.make_async_copy(ref, ref, ag_own.at[par, flow, px * NY + py]).wait()
        to_partner(par, flow, px, py)

    def oriented(flow):
        if flow == 0:
            return (x, xr, xl, xo), (y, yr, yl, yo), "x", "y"
        return (y, yr, yl, yo), (x, xr, xl, xo), "y", "x"

    def at(flow, a, b):
        return (a, b) if flow == 0 else (b, a)

    def gather_own(par):
        for flow in range(2):
            (a, ar, al, ao), (b, br, bl, bo), an, bn = oriented(flow)
            for c in (ao, ar, al):
                push(par, flow, *at(flow, a, b), **{an: c})
        for flow in range(2):
            (a, ar, al, ao), (b, br, bl, bo), an, bn = oriented(flow)
            for c in (br, bl):
                push(par, flow, *at(flow, a, b), **{bn: c})
        for flow in range(2):
            to_partner(par, flow, x, y)

    def onward(par, hop):
        for flow in range(2):
            firsts, (b, br, bl, bo), an, bn = oriented(flow)
            arrived(par, flow, *at(flow, firsts[hop], b))
            for c in (br, bl):
                push(par, flow, *at(flow, firsts[hop], b), **{bn: c})

    def across(par, hop):
        for flow in range(2):
            firsts, (b, br, bl, bo), an, bn = oriented(flow)
            a = firsts[hop]
            arrived(par, flow, *at(flow, a, bl))
            push(par, flow, *at(flow, a, bl), piece=0, **{bn: br})
            arrived(par, flow, *at(flow, a, br))
            push(par, flow, *at(flow, a, br), piece=1, **{bn: bl})

    def gather_last(par):
        for hop in range(4):
            for flow in range(2):
                firsts, (b, br, bl, bo), an, bn = oriented(flow)
                arrived(par, flow, *at(flow, firsts[hop], bo))

    def gather_end(par):
        for flow in range(2):
            for px in range(NX):
                for py in range(NY):
                    ref = block(par, flow, px, py, core=kp)
                    pltpu.make_async_copy(ref, ref, ag_par.at[par, flow, px * NY + py]).wait()
        sent = gat[par].at[pl.ds(0, 62)]
        pltpu.make_async_copy(sent, sent, ag_send).wait()

    def set_basis(par, values):
        for j in range(2):
            gat[par][place(j, k, x, y)] = (scale[j] * values[j]).astype(BF16)

    def total(buf, par, count):
        terms = [buf[par, i] for i in range(count)]
        while len(terms) > 1:
            terms = [terms[i] + terms[i + 1] for i in range(0, len(terms), 2)]
        return terms[0]

    def gram_send(par):
        zbuf[par, me_kz] = gram[me_kz]
        for pk, pz in kz_peers:
            remote(gram.at[pk * NZ + pz], zbuf.at[par, me_kz], ar_send.at[0], zsem.at[par, me_kz], k=pk, z=pz).start()

    def wait_for(ref, sem):
        pltpu.make_async_copy(ref, ref, sem).wait()

    def gram_plane(par):
        for pk, pz in kz_peers:
            wait_for(zbuf.at[par, pk * NZ + pz], zsem.at[par, pk * NZ + pz])
        xybuf[par, me_xy] = total(zbuf, par, NK * NZ)
        for px, py in xy_peers:
            mine = xybuf.at[par, me_xy]
            remote(mine, mine, ar_send.at[1], xysem.at[par, me_xy], x=px, y=py).start()

    def gram_all(par):
        for px, py in xy_peers:
            wait_for(xybuf.at[par, px * NY + py], xysem.at[par, px * NY + py])
        gfull[par, me_kz] = total(xybuf, par, NX * NY)
        for pk, pz in kz_peers:
            mine = gfull.at[par, me_kz]
            remote(mine, mine, ar_send.at[2], fsem.at[par, me_kz], k=pk, z=pz).start()

    def gram_end(par):
        for pk, pz in kz_peers:
            wait_for(gfull.at[par, pk * NZ + pz], fsem.at[par, pk * NZ + pz])
        wait_for(gram.at[pl.ds(0, 7)], ar_send.at[0])
        wait_for(xybuf.at[par, pl.ds(0, 15)], ar_send.at[1])
        wait_for(gfull.at[par, pl.ds(0, 7)], ar_send.at[2])

    npts = NX * NY * NK * NZ * 2 * TILE
    panel = 16
    lane_id = lax.broadcasted_iota(jnp.int32, (WIDTH, WIDTH), 1)
    row_id = lax.broadcasted_iota(jnp.int32, (WIDTH, WIDTH), 0)
    sub_id = lax.broadcasted_iota(jnp.int32, (8, WIDTH), 0)

    def outer(rows):
        high = rows.astype(BF16)
        rest = rows - high.astype(F32)
        mid = rest.astype(BF16)
        low = (rest - mid.astype(F32)).astype(BF16)
        a = jnp.concatenate([high, high, mid, mid, high, low], axis=0)
        b = jnp.concatenate([high, mid, high, mid, low, high], axis=0)
        return contract(a[:, 0:WIDTH], b, 0, 0)

    def eliminate(base):
        rows = [aug[pl.ds(base + r, 8, stride=0), :] for r in range(panel)]
        d = {
            (r, c): jnp.broadcast_to(rows[r][:, base + c : base + c + 1], (8, WIDTH))
            for r in range(panel) for c in range(r, panel)
        }
        inv, low = [], {}
        for j in range(panel):
            inv.append(lax.rsqrt(d[j, j]))
            for c in range(j + 1, panel):
                low[c, j] = d[j, c] * inv[j]
            for r in range(j + 1, panel):
                for c in range(r, panel):
                    d[r, c] = d[r, c] - low[r, j] * low[c, j]
        done = []
        for j in range(panel):
            left, right = rows[j][:, 0:WIDTH], rows[j][:, WIDTH:]
            for i in range(j):
                left = left - low[j, i] * done[i][0]
                right = right - low[j, i] * done[i][1]
            done.append((left * inv[j], right * inv[j]))
        groups = []
        for o in range(0, panel, 8):
            sides = []
            for side in range(2):
                v = done[o][side]
                for j in range(1, 8):
                    v = jnp.where(sub_id == j, done[o + j][side], v)
                sides.append(v)
            groups.append(jnp.concatenate(sides, axis=1))
        return jnp.concatenate(groups, axis=0)

    def eliminate_rows(first, last):
        for base in range(first, last, panel):
            rows = eliminate(base)
            aug[base : base + panel, :] = rows
            after = base + panel
            if after < WIDTH:
                aug[after:, :] = aug[after:, :] - outer(rows)[after:, :]

    def factor_top(par):
        aug[:, 0:WIDTH] = gfull[par].reshape(WIDTH, WIDTH) * (1.0 / npts)
        aug[:, WIDTH:] = jnp.where(row_id == lane_id, 1.0, 0.0).astype(F32)
        eliminate_rows(0, SPLITS[0])

    def factor_middle(par):
        eliminate_rows(SPLITS[0], SPLITS[1])

    def factor_rest(par):
        eliminate_rows(SPLITS[1], WIDTH)
        linv[...] = aug[:, WIDTH:]

    set_basis(0, basis[...].astype(F32).reshape(2, TILE, WIDTH))
    gather_own(0)
    for hop in (1, 2, 3):
        onward(0, hop)
    for hop in range(4):
        across(0, hop)
    gather_last(0)
    gather_end(0)
    linv[...] = jnp.where(
        lax.broadcasted_iota(jnp.int32, (WIDTH, WIDTH), 0)
        == lax.broadcasted_iota(jnp.int32, (WIDTH, WIDTH), 1), 1.0, 0.0,
    ).astype(F32)
    for pz in z_peers:
        wait_for(recv.at[part(pz * Q, Q)], tile_recv.at[pz])
    for c in tile_copies:
        c.wait_send()

    def multiply(par):
        product = None
        for g in range(NZ):
            left, right = [], []
            for q in range(Q):
                s = g * Q + q
                fetch = slot_fetch[0, s]
                where = (mod(fetch, 2) * 2 + fetch_list[0, fetch]) * (NX * NY) + fetch // 2
                u = gat[par][where]
                row = slot_row[0, s]
                zero = jnp.zeros_like(u)
                left.append(recv[s])
                right.append(
                    jnp.concatenate([jnp.where(row == 0, u, zero), jnp.where(row == 1, u, zero)], axis=1)
                )
            term = jnp.dot(
                jnp.concatenate(left, axis=1), jnp.concatenate(right, axis=0),
                preferred_element_type=F32,
            )
            product = term if product is None else product + term
        acc[...] = product

    def iteration(now, more):
        later = 1 - now
        for j in range(2):
            ybuf[j] = contract(scale[j] * acc[:, j * WIDTH : (j + 1) * WIDTH], linv[...], 1, 1, HI)
        local = contract(ybuf[0], ybuf[0], 0, 0, HI) + contract(ybuf[1], ybuf[1], 0, 0, HI)
        gram[...] = local.reshape(NK * NZ, WIDTH // (NK * NZ), WIDTH)

        def when_more(body):
            if more is True:
                body()
            else:
                pl.when(more)(body)

        steps = {
            "basis": lambda: set_basis(later, ybuf),
            "own": lambda: gather_own(later),
            "last": lambda: gather_last(later),
        }
        for hop in range(4):
            steps[f"on{hop}"] = functools.partial(onward, later, hop)
            steps[f"x{hop}"] = functools.partial(across, later, hop)
        sums = {
            "send": gram_send, "plane": gram_plane, "all": gram_all, "sum": gram_end,
            "top": factor_top, "middle": factor_middle,
        }
        waiting = []

        def flush():
            todo = list(waiting)
            waiting.clear()

            def body():
                for name in todo:
                    steps[name]()

            if todo:
                when_more(body)

        for name in ORDER:
            if name in sums:
                flush()
                sums[name](later)
            else:
                waiting.append(name)
        flush()

        def both():
            gather_end(later)
            factor_rest(later)
            multiply(later)

        when_more(both)
        if more is not True:
            pl.when(jnp.logical_not(more))(lambda: factor_rest(later))

    def pair(i, carry):
        iteration(0, True)
        iteration(1, i < ITERS // 2 - 1)
        return carry

    multiply(0)
    lax.fori_loop(0, ITERS // 2, pair, 0)
    for j in range(2):
        out[j * TILE : (j + 1) * TILE, :] = contract(ybuf[j], linv[...], 1, 1, HI).astype(BF16)


def on_device(tiles, send_slot, slot_row, slot_fetch, fetch_list, basis):
    dma = pltpu.SemaphoreType.DMA
    vmem = pltpu.VMEM
    chunk = WIDTH // (NK * NZ)
    return pl.pallas_call(
        kernel,
        out_shape=jax.ShapeDtypeStruct(basis.shape, BF16),
        in_specs=[
            pl.BlockSpec(memory_space=pltpu.SMEM),
            pl.BlockSpec(memory_space=pltpu.SMEM),
            pl.BlockSpec(memory_space=pltpu.SMEM),
            pl.BlockSpec(memory_space=pltpu.SMEM),
            pl.BlockSpec(memory_space=pl.ANY),
            pl.BlockSpec(memory_space=pltpu.VMEM),
        ],
        out_specs=pl.BlockSpec(memory_space=pltpu.VMEM),
        scratch_shapes=[
            pltpu.SMEM((SLOTS,), jnp.int32),
            vmem((SLOTS, TILE, TILE), BF16),
            vmem((SLOTS, TILE, TILE), BF16),
            vmem((SLOTS, TILE, TILE), BF16),
            vmem((NZ, Q, TILE), F32),
            vmem((NZ, Q, TILE), F32),
            vmem((2, SLOTS, WIDTH), F32),
            vmem((2, TILE, WIDTH), F32),
            vmem((2 * NX * NY * NK, TILE, WIDTH), BF16),
            vmem((2 * NX * NY * NK, TILE, WIDTH), BF16),
            vmem((2, TILE, WIDTH), F32),
            vmem((TILE, 2 * WIDTH), F32),
            vmem((NK * NZ, chunk, WIDTH), F32),
            vmem((2, NK * NZ, chunk, WIDTH), F32),
            vmem((2, NX * NY, chunk, WIDTH), F32),
            vmem((2, NK * NZ, chunk, WIDTH), F32),
            vmem((WIDTH, 2 * WIDTH), F32),
            vmem((WIDTH, WIDTH), F32),
            dma, dma((5,)), dma((NZ,)), dma((NZ - 1,)), dma((NZ,)),
            dma, dma((2, 2, NX * NY)), dma((2, 2, NX * NY)),
            dma((3,)), dma((2, NK * NZ)), dma((2, NX * NY)), dma((2, NK * NZ)),
        ],
        compiler_params=pltpu.CompilerParams(collective_id=0, has_side_effects=True),
    )(send_slot, slot_row, slot_fetch, fetch_list, tiles, basis)


def solution(mesh):
    split = Mesh(mesh.devices.reshape(NX, NY, NK, NZ), AXES)
    return jax.shard_map(
        on_device,
        mesh=split,
        in_specs=(P(AXES, None, None),) + (P(AXES, None),) * 5,
        out_specs=P(AXES, None),
        check_vma=False,
    )
```

```python
import functools

import jax
import jax.numpy as jnp
from jax import lax
from jax.experimental import pallas as pl
from jax.experimental.pallas import tpu as pltpu
from jax.sharding import Mesh
from jax.sharding import PartitionSpec as P

TILE = 256
WIDTH = 128
ITERS = 6
NX, NY, NK, NZ = 4, 4, 2, 4
Q = 8
SLOTS = NZ * Q
AXES = ("x", "y", "k", "z")
MESH = pl.DeviceIdType.MESH
HI = lax.Precision.HIGHEST
F32 = jnp.float32
BF16 = jnp.bfloat16
ORDER = (
    "basis", "own", "send", "plane", "on1", "on2", "on3", "x0", "all",
    "x1", "x2", "x3", "sum", "top", "last", "middle",
)
SPLITS = (80, 112)


def contract(a, b, da, db, precision=None):
    return lax.dot_general(
        a, b, (((da,), (db,)), ((), ())), precision=precision, preferred_element_type=F32
    )


def kernel(
    send_slot, slot_row, slot_fetch, fetch_list, tiles, basis, out,
    source, tin, stg, recv, rsend, rrecv, mrow, scale, gat_even, gat_odd, ybuf, acc,
    gram, zbuf, xybuf, gfull, aug, linv,
    in_sem, tile_send, tile_recv, row_send, row_recv,
    ag_send, ag_own, ag_par, ar_send, zsem, xysem, fsem,
):
    x, y, k, z = (lax.axis_index(a) for a in AXES)
    mod = lax.rem
    xr, xl, xo = mod(x + 1, NX), mod(x + 3, NX), mod(x + 2, NX)
    yr, yl, yo = mod(y + 1, NY), mod(y + 3, NY), mod(y + 2, NY)
    zr, zl, zo = mod(z + 1, NZ), mod(z + 3, NZ), mod(z + 2, NZ)
    kp = 1 - k
    kz_peers = [
        (mod(k + dk, NK), mod(z + dz, NZ))
        for dz in (2, 1, 3, 0) for dk in (1, 0) if (dk, dz) != (0, 0)
    ]
    xy_peers = [
        (mod(x + dx, NX), mod(y + dy, NY))
        for dx in (2, 1, 3, 0) for dy in (2, 1, 3, 0) if (dx, dy) != (0, 0)
    ]
    z_peers = (zo, zr, zl)
    me_xy = x * NY + y
    me_kz = k * NZ + z

    def remote(src, dst, ssem, rsem, **dev):
        return pltpu.make_async_remote_copy(
            src_ref=src, dst_ref=dst, send_sem=ssem, recv_sem=rsem,
            device_id=dev, device_id_type=MESH,
        )

    load_tiles = pltpu.make_async_copy(tiles, tin, in_sem)
    load_tiles.start()

    barrier = pltpu.get_barrier_semaphore()
    for pk, pz in kz_peers:
        pl.semaphore_signal(barrier, inc=1, device_id={"k": pk, "z": pz}, device_id_type=MESH)
    for px, py in xy_peers:
        pl.semaphore_signal(barrier, inc=1, device_id={"x": px, "y": py}, device_id_type=MESH)

    def find_tile(slot, carry):
        tile = jnp.int32(0)
        for t in range(SLOTS):
            tile = jnp.where(send_slot[0, t] == slot, t, tile)
        source[slot] = tile
        return carry

    lax.fori_loop(0, SLOTS, find_tile, 0)
    for s in range(SLOTS):
        for j in range(2):
            hit = jnp.where(slot_row[0, s] == j, 1.0, 0.0).astype(F32)
            mrow[j, s : s + 1, :] = jnp.full((1, WIDTH), hit, F32)
    load_tiles.wait()

    ones = jnp.ones((8, TILE), BF16)

    def part(start, count):
        return pl.ds(start, count)

    def put_in_order(d):
        for q in range(Q):
            stg[d * Q + q] = tin[source[d * Q + q]]

    def send_tiles(i, pz, first, count):
        c = remote(
            stg.at[part(pz * Q + first, count)], recv.at[part(z * Q + first, count)],
            tile_send.at[i], tile_recv.at[z], z=pz,
        )
        c.start()
        return c

    few = 2
    put_in_order(zr)
    put_in_order(zl)
    pl.semaphore_wait(barrier, len(kz_peers) + len(xy_peers))
    tile_copies = [send_tiles(0, zr, 0, few), send_tiles(1, zl, 0, few)]
    put_in_order(zo)
    put_in_order(z)

    def sum_rows(d, carry):
        for q in range(Q):
            t = jnp.abs(stg[d * Q + q])
            rsend[d, q : q + 1, :] = contract(ones, t, 1, 1)[0:1]
        return carry

    lax.fori_loop(0, NZ, sum_rows, 0)
    row_copies = [
        remote(rsend.at[pz], rrecv.at[z], row_send.at[i], row_recv.at[z], z=pz)
        for i, pz in enumerate(z_peers)
    ]
    for c in row_copies:
        c.start()
    tile_copies += [
        send_tiles(2, zo, 0, Q), send_tiles(3, zr, few, Q - few), send_tiles(4, zl, few, Q - few)
    ]
    for q in range(Q):
        recv[z * Q + q] = stg[z * Q + q]
    rrecv[z] = rsend[z]
    for pz in z_peers:
        pltpu.make_async_copy(rrecv.at[pz], rrecv.at[pz], row_recv.at[pz]).wait()
    for c in row_copies:
        c.wait_send()
    rows = rrecv[...].reshape(SLOTS, TILE)
    for j in range(2):
        scale[j] = lax.rsqrt(1.0 + contract(rows, mrow[j], 0, 0, HI))

    gat = (gat_even, gat_odd)

    def place(flow, core, px, py):
        return ((core * 2 + flow) * NX + px) * NY + py

    def block(par, flow, px, py, piece=None, core=None):
        ref = gat[par].at[place(flow, k if core is None else core, px, py)]
        return ref if piece is None else ref.at[pl.ds(piece * (TILE // 2), TILE // 2)]

    def push(par, flow, px, py, piece=None, **dev):
        ref = block(par, flow, px, py, piece)
        remote(ref, ref, ag_send, ag_own.at[par, flow, px * NY + py], **dev).start()

    def to_partner(par, flow, px, py):
        ref = block(par, flow, px, py)
        remote(ref, ref, ag_send, ag_par.at[par, flow, px * NY + py], k=kp).start()

    def arrived(par, flow, px, py):
        ref = block(par, flow, px, py)
        pltpu.make_async_copy(ref, ref, ag_own.at[par, flow, px * NY + py]).wait()
        to_partner(par, flow, px, py)

    def oriented(flow):
        if flow == 0:
            return (x, xr, xl, xo), (y, yr, yl, yo), "x", "y"
        return (y, yr, yl, yo), (x, xr, xl, xo), "y", "x"

    def at(flow, a, b):
        return (a, b) if flow == 0 else (b, a)

    def gather_own(par):
        for flow in range(2):
            (a, ar, al, ao), (b, br, bl, bo), an, bn = oriented(flow)
            for c in (ao, ar, al):
                push(par, flow, *at(flow, a, b), **{an: c})
        for flow in range(2):
            (a, ar, al, ao), (b, br, bl, bo), an, bn = oriented(flow)
            for c in (br, bl):
                push(par, flow, *at(flow, a, b), **{bn: c})
        for flow in range(2):
            to_partner(par, flow, x, y)

    def onward(par, hop):
        for flow in range(2):
            firsts, (b, br, bl, bo), an, bn = oriented(flow)
            arrived(par, flow, *at(flow, firsts[hop], b))
            for c in (br, bl):
                push(par, flow, *at(flow, firsts[hop], b), **{bn: c})

    def across(par, hop):
        for flow in range(2):
            firsts, (b, br, bl, bo), an, bn = oriented(flow)
            a = firsts[hop]
            arrived(par, flow, *at(flow, a, bl))
            push(par, flow, *at(flow, a, bl), piece=0, **{bn: br})
            arrived(par, flow, *at(flow, a, br))
            push(par, flow, *at(flow, a, br), piece=1, **{bn: bl})

    def gather_last(par):
        for hop in range(4):
            for flow in range(2):
                firsts, (b, br, bl, bo), an, bn = oriented(flow)
                arrived(par, flow, *at(flow, firsts[hop], bo))

    def gather_end(par):
        for flow in range(2):
            for px in range(NX):
                for py in range(NY):
                    ref = block(par, flow, px, py, core=kp)
                    pltpu.make_async_copy(ref, ref, ag_par.at[par, flow, px * NY + py]).wait()
        sent = gat[par].at[pl.ds(0, 62)]
        pltpu.make_async_copy(sent, sent, ag_send).wait()

    def set_basis(par, values):
        for j in range(2):
            gat[par][place(j, k, x, y)] = (scale[j] * values[j]).astype(BF16)

    def total(buf, par, count):
        terms = [buf[par, i] for i in range(count)]
        while len(terms) > 1:
            terms = [terms[i] + terms[i + 1] for i in range(0, len(terms), 2)]
        return terms[0]

    def gram_send(par):
        zbuf[par, me_kz] = gram[me_kz]
        for pk, pz in kz_peers:
            remote(gram.at[pk * NZ + pz], zbuf.at[par, me_kz], ar_send.at[0], zsem.at[par, me_kz], k=pk, z=pz).start()

    def wait_for(ref, sem):
        pltpu.make_async_copy(ref, ref, sem).wait()

    def gram_plane(par):
        for pk, pz in kz_peers:
            wait_for(zbuf.at[par, pk * NZ + pz], zsem.at[par, pk * NZ + pz])
        xybuf[par, me_xy] = total(zbuf, par, NK * NZ)
        for px, py in xy_peers:
            mine = xybuf.at[par, me_xy]
            remote(mine, mine, ar_send.at[1], xysem.at[par, me_xy], x=px, y=py).start()

    def gram_all(par):
        for px, py in xy_peers:
            wait_for(xybuf.at[par, px * NY + py], xysem.at[par, px * NY + py])
        gfull[par, me_kz] = total(xybuf, par, NX * NY)
        for pk, pz in kz_peers:
            mine = gfull.at[par, me_kz]
            remote(mine, mine, ar_send.at[2], fsem.at[par, me_kz], k=pk, z=pz).start()

    def gram_end(par):
        for pk, pz in kz_peers:
            wait_for(gfull.at[par, pk * NZ + pz], fsem.at[par, pk * NZ + pz])
        wait_for(gram.at[pl.ds(0, 7)], ar_send.at[0])
        wait_for(xybuf.at[par, pl.ds(0, 15)], ar_send.at[1])
        wait_for(gfull.at[par, pl.ds(0, 7)], ar_send.at[2])

    npts = NX * NY * NK * NZ * 2 * TILE
    panel = 16
    lane_id = lax.broadcasted_iota(jnp.int32, (WIDTH, WIDTH), 1)
    row_id = lax.broadcasted_iota(jnp.int32, (WIDTH, WIDTH), 0)
    sub_id = lax.broadcasted_iota(jnp.int32, (8, WIDTH), 0)

    def outer(rows):
        high = rows.astype(BF16)
        rest = rows - high.astype(F32)
        mid = rest.astype(BF16)
        low = (rest - mid.astype(F32)).astype(BF16)
        a = jnp.concatenate([high, high, mid, mid, high, low], axis=0)
        b = jnp.concatenate([high, mid, high, mid, low, high], axis=0)
        return contract(a[:, 0:WIDTH], b, 0, 0)

    def eliminate(base):
        rows = [aug[pl.ds(base + r, 8, stride=0), :] for r in range(panel)]
        d = {
            (r, c): jnp.broadcast_to(rows[r][:, base + c : base + c + 1], (8, WIDTH))
            for r in range(panel) for c in range(r, panel)
        }
        inv, low = [], {}
        for j in range(panel):
            inv.append(lax.rsqrt(d[j, j]))
            for c in range(j + 1, panel):
                low[c, j] = d[j, c] * inv[j]
            for r in range(j + 1, panel):
                for c in range(r, panel):
                    d[r, c] = d[r, c] - low[r, j] * low[c, j]
        done = []
        for j in range(panel):
            left, right = rows[j][:, 0:WIDTH], rows[j][:, WIDTH:]
            for i in range(j):
                left = left - low[j, i] * done[i][0]
                right = right - low[j, i] * done[i][1]
            done.append((left * inv[j], right * inv[j]))
        groups = []
        for o in range(0, panel, 8):
            sides = []
            for side in range(2):
                v = done[o][side]
                for j in range(1, 8):
                    v = jnp.where(sub_id == j, done[o + j][side], v)
                sides.append(v)
            groups.append(jnp.concatenate(sides, axis=1))
        return jnp.concatenate(groups, axis=0)

    def eliminate_rows(first, last):
        for base in range(first, last, panel):
            rows = eliminate(base)
            aug[base : base + panel, :] = rows
            after = base + panel
            if after < WIDTH:
                aug[after:, :] = aug[after:, :] - outer(rows)[after:, :]

    def factor_top(par):
        aug[:, 0:WIDTH] = gfull[par].reshape(WIDTH, WIDTH) * (1.0 / npts)
        aug[:, WIDTH:] = jnp.where(row_id == lane_id, 1.0, 0.0).astype(F32)
        eliminate_rows(0, SPLITS[0])

    def factor_middle(par):
        eliminate_rows(SPLITS[0], SPLITS[1])

    def factor_rest(par):
        eliminate_rows(SPLITS[1], WIDTH)
        linv[...] = aug[:, WIDTH:]

    set_basis(0, basis[...].astype(F32).reshape(2, TILE, WIDTH))
    gather_own(0)
    for hop in (1, 2, 3):
        onward(0, hop)
    for hop in range(4):
        across(0, hop)
    gather_last(0)
    gather_end(0)
    linv[...] = jnp.where(
        lax.broadcasted_iota(jnp.int32, (WIDTH, WIDTH), 0)
        == lax.broadcasted_iota(jnp.int32, (WIDTH, WIDTH), 1), 1.0, 0.0,
    ).astype(F32)
    for pz in z_peers:
        wait_for(recv.at[part(pz * Q, Q)], tile_recv.at[pz])
    for c in tile_copies:
        c.wait_send()

    def multiply(par):
        product = None
        for g in range(NZ):
            left, right = [], []
            for q in range(Q):
                s = g * Q + q
                fetch = slot_fetch[0, s]
                where = (mod(fetch, 2) * 2 + fetch_list[0, fetch]) * (NX * NY) + fetch // 2
                u = gat[par][where]
                row = slot_row[0, s]
                zero = jnp.zeros_like(u)
                left.append(recv[s])
                right.append(
                    jnp.concatenate([jnp.where(row == 0, u, zero), jnp.where(row == 1, u, zero)], axis=1)
                )
            term = jnp.dot(
                jnp.concatenate(left, axis=1), jnp.concatenate(right, axis=0),
                preferred_element_type=F32,
            )
            product = term if product is None else product + term
        acc[...] = product

    def gram_local(par):
        local = contract(ybuf[0], ybuf[0], 0, 0, HI) + contract(ybuf[1], ybuf[1], 0, 0, HI)
        gram[...] = local.reshape(NK * NZ, WIDTH // (NK * NZ), WIDTH)
        gram_send(par)

    def iteration(now, more):
        later = 1 - now
        for j in range(2):
            ybuf[j] = contract(scale[j] * acc[:, j * WIDTH : (j + 1) * WIDTH], linv[...], 1, 1, HI)

        def when_more(body):
            if more is True:
                body()
            else:
                pl.when(more)(body)

        steps = {
            "basis": lambda: set_basis(later, ybuf),
            "own": lambda: gather_own(later),
            "last": lambda: gather_last(later),
        }
        for hop in range(4):
            steps[f"on{hop}"] = functools.partial(onward, later, hop)
            steps[f"x{hop}"] = functools.partial(across, later, hop)
        sums = {
            "send": gram_local, "plane": gram_plane, "all": gram_all, "sum": gram_end,
            "top": factor_top, "middle": factor_middle,
        }
        waiting = []

        def flush():
            todo = list(waiting)
            waiting.clear()

            def body():
                for name in todo:
                    steps[name]()

            if todo:
                when_more(body)

        for name in ORDER:
            if name in sums:
                flush()
                sums[name](later)
            else:
                waiting.append(name)
        flush()

        def both():
            gather_end(later)
            factor_rest(later)
            multiply(later)

        when_more(both)
        if more is not True:
            pl.when(jnp.logical_not(more))(lambda: factor_rest(later))

    def pair(i, carry):
        iteration(0, True)
        iteration(1, i < ITERS // 2 - 1)
        return carry

    multiply(0)
    lax.fori_loop(0, ITERS // 2, pair, 0)
    for j in range(2):
        out[j * TILE : (j + 1) * TILE, :] = contract(ybuf[j], linv[...], 1, 1, HI).astype(BF16)


def on_device(tiles, send_slot, slot_row, slot_fetch, fetch_list, basis):
    dma = pltpu.SemaphoreType.DMA
    vmem = pltpu.VMEM
    chunk = WIDTH // (NK * NZ)
    return pl.pallas_call(
        kernel,
        out_shape=jax.ShapeDtypeStruct(basis.shape, BF16),
        in_specs=[
            pl.BlockSpec(memory_space=pltpu.SMEM),
            pl.BlockSpec(memory_space=pltpu.SMEM),
            pl.BlockSpec(memory_space=pltpu.SMEM),
            pl.BlockSpec(memory_space=pltpu.SMEM),
            pl.BlockSpec(memory_space=pl.ANY),
            pl.BlockSpec(memory_space=pltpu.VMEM),
        ],
        out_specs=pl.BlockSpec(memory_space=pltpu.VMEM),
        scratch_shapes=[
            pltpu.SMEM((SLOTS,), jnp.int32),
            vmem((SLOTS, TILE, TILE), BF16),
            vmem((SLOTS, TILE, TILE), BF16),
            vmem((SLOTS, TILE, TILE), BF16),
            vmem((NZ, Q, TILE), F32),
            vmem((NZ, Q, TILE), F32),
            vmem((2, SLOTS, WIDTH), F32),
            vmem((2, TILE, WIDTH), F32),
            vmem((2 * NX * NY * NK, TILE, WIDTH), BF16),
            vmem((2 * NX * NY * NK, TILE, WIDTH), BF16),
            vmem((2, TILE, WIDTH), F32),
            vmem((TILE, 2 * WIDTH), F32),
            vmem((NK * NZ, chunk, WIDTH), F32),
            vmem((2, NK * NZ, chunk, WIDTH), F32),
            vmem((2, NX * NY, chunk, WIDTH), F32),
            vmem((2, NK * NZ, chunk, WIDTH), F32),
            vmem((WIDTH, 2 * WIDTH), F32),
            vmem((WIDTH, WIDTH), F32),
            dma, dma((5,)), dma((NZ,)), dma((NZ - 1,)), dma((NZ,)),
            dma, dma((2, 2, NX * NY)), dma((2, 2, NX * NY)),
            dma((3,)), dma((2, NK * NZ)), dma((2, NX * NY)), dma((2, NK * NZ)),
        ],
        compiler_params=pltpu.CompilerParams(collective_id=0, has_side_effects=True),
    )(send_slot, slot_row, slot_fetch, fetch_list, tiles, basis)


def solution(mesh):
    split = Mesh(mesh.devices.reshape(NX, NY, NK, NZ), AXES)
    return jax.shard_map(
        on_device,
        mesh=split,
        in_specs=(P(AXES, None, None),) + (P(AXES, None),) * 5,
        out_specs=P(AXES, None),
        check_vma=False,
    )
```
